512 devices in a mesh: quad: 16 (over z_lo, core), gy: 8 (over y, z_hi), gx: 4 (over x).
Axes of the slice: x: 4, y: 4, z: 16 (z_hi: 2, z_lo: 8; z = z_hi * 8 + z_lo), core: 2. Of those that a mesh axis runs over, the one named last changes fastest.
Arguments:
- modes_now: bfloat16 [1024, 64, 512], P('quad', 'gy', 'gx'), may hold values from -4 to 4
- basis_rows: bfloat16 [4096, 1024], P('quad'), may hold values from -0.25 to 0.25
- quad_weights: float32 [4096], P('quad'), may hold values from 0.2 to 2
- germ_nodes: float32 [4096, 8], P('quad'), may hold values from -1.5 to 1.5
- log_fields: float32 [8, 64, 512], P(None, 'gy', 'gx'), may hold values from -1 to 1
- reaction_rates: float32 [4096], P('quad'), may hold values from 0.08 to 0.32
Outputs:
- modes_next: float32 [1024, 64, 512], P('quad', 'gy', 'gx')
The draws below stay inside these ranges and needn't reach their ends.
All inputs are finite; a program needn't handle non-finite values.
Results may differ from the reference program's by a relative error of at most 0.02.
Values may be sent and summed in bfloat16 or wider, within the bound.
No kernel may reach another device: no remote copies, remote signals or barrier semaphores. Data moves between devices by JAX's collectives and lax.ppermute only.
A program may use at most 64 MiB of HBM per device.

```python
import math
import jax
import jax.numpy as jnp
from jax import lax

MODES = 1024
QUAD_PTS = 4096
TERMS = 8
NY = 64
NX = 512
N_QUAD = 16


def strengthened(drawn, rng, source, target, parts, factor):
    owner, partner = [(jnp.arange(drawn.shape[dim]) // (drawn.shape[dim] // parts)).reshape([-1 if axis == dim else 1 for axis in range(drawn.ndim)]) for dim in (source, target)]
    chosen = jax.random.permutation(rng, parts)[partner]
    strong = (owner == chosen) | (owner == (partner + parts // 2) % parts)
    return jnp.where(strong, factor * drawn, drawn)


def levels(key, shape, shards, smallest, largest):
    def one(dim, parts):
        draws = jax.random.uniform(jax.random.fold_in(jax.random.fold_in(key, 6), dim), (parts,), jnp.float32, smallest / len(shards), largest / len(shards))
        return jnp.repeat(jnp.exp(draws), shape[dim] // parts).reshape((-1,) + (1,) * (len(shape) - dim - 1))

    loudness = one(*shards[0])
    for cut in shards[1:]:
        loudness = loudness * one(*cut)
    return loudness


def noise(key, shape, deviation, most, pieces=(), kind=jnp.bfloat16):
    entries = deviation * jax.random.normal(key, shape, jnp.float32)
    if pieces:
        entries = entries * levels(key, shape, pieces, -0.22, 0.18)
    return jnp.clip(entries, -most, most).astype(kind)


def noise_with(key, dims, width, bound, cuts, heavy, kind=jnp.bfloat16):
    entries = width * jax.random.normal(key, dims, jnp.float32)
    if cuts:
        entries = entries * levels(key, dims, cuts, -0.22, 0.18)
    return jnp.clip(strengthened(entries, jax.random.fold_in(key, 3), *heavy), -bound, bound).astype(kind)


def setup_inputs(seed: int = 0) -> dict:
    keys = jax.random.split(jax.random.key(seed), 7)
    return {
        "modes_now": noise(keys[0], (MODES, NY, NX), 1.0, 4.0, ((0, 16), (1, 8), (2, 4))),
        "basis_rows": noise_with(keys[1], (QUAD_PTS, MODES), MODES ** -0.5, 0.25, ((0, 16),), (0, 1, 16, 2.0)),
        "quad_weights": jnp.clip(jnp.exp(math.log(2.0) - 2.3025851 * jax.random.uniform(keys[2], (QUAD_PTS,), jnp.float32) ** levels(keys[2], (QUAD_PTS,), ((0, 16),), -0.2, 0.2)), 0.2, 2.0),
        "germ_nodes": jnp.clip(jax.random.uniform(keys[3], (QUAD_PTS, TERMS), jnp.float32, -1.5, 1.5) * levels(keys[3], (QUAD_PTS, TERMS), ((0, 16),), -0.4, 0.0), -1.5, 1.5),
        "log_fields": jnp.clip(jax.random.uniform(keys[4], (TERMS, NY, NX), jnp.float32, -1.0, 1.0) * levels(keys[4], (TERMS, NY, NX), ((1, 8), (2, 4)), -0.4, 0.0), -1.0, 1.0),
        "reaction_rates": jnp.clip(jnp.exp(math.log(0.32) - 1.3862944 * jax.random.uniform(keys[5], (QUAD_PTS,), jnp.float32) ** levels(keys[5], (QUAD_PTS,), ((0, 16),), -0.2, 0.2)), 0.08, 0.32),
    }


def neighbour(array, drow, dcol):
    return array[:, 1 + drow:array.shape[1] - 1 + drow, 1 + dcol:array.shape[2] - 1 + dcol]


def drive_of(field_ext, coeff_ext, rates, weights):
    center = neighbour(field_ext, 0, 0)
    coeff_mid = neighbour(coeff_ext, 0, 0)
    total = jnp.zeros_like(center)
    for drow, dcol in ((-1, 0), (1, 0), (0, -1), (0, 1)):
        total = total + (coeff_mid + neighbour(coeff_ext, drow, dcol)) * (neighbour(field_ext, drow, dcol) - center)
    total = total + rates[:, None, None] * (center - center * center * center)
    return (weights[:, None, None] * total).astype(jnp.bfloat16)


def project(iterate, basis_rows, quad_weights, germ_nodes, log_padded, reaction_rates):
    q_group = QUAD_PTS // N_QUAD
    flat = iterate.reshape(MODES, -1)

    def group(total, index):
        first = (index * q_group).astype(jnp.int32)
        rows = lax.dynamic_slice_in_dim(basis_rows, first, q_group, 0)
        nodes = lax.dynamic_slice_in_dim(germ_nodes, first, q_group, 0)
        weights = lax.dynamic_slice_in_dim(quad_weights, first, q_group, 0)
        rates = lax.dynamic_slice_in_dim(reaction_rates, first, q_group, 0)
        field = jnp.dot(rows, flat, preferred_element_type=jnp.float32).reshape(q_group, NY, NX)
        field_ext = jnp.pad(field, ((0, 0), (1, 1), (1, 1)))
        coeff_ext = jnp.exp(jnp.einsum("qj,jyx->qyx", nodes, log_padded, precision=lax.Precision.HIGHEST))
        weighted = drive_of(field_ext, coeff_ext, rates, weights).reshape(q_group, -1)
        part = lax.dot_general(rows, weighted, (((0,), (0,)), ((), ())), preferred_element_type=jnp.float32)
        rounded = lax.optimization_barrier(part.astype(jnp.bfloat16))
        return total + rounded.astype(jnp.float32), None

    start = jnp.zeros((MODES, NY * NX), jnp.float32)
    total, _ = lax.scan(group, start, jnp.arange(N_QUAD, dtype=jnp.int32))
    return total.reshape(MODES, NY, NX)


def reference(modes_now, basis_rows, quad_weights, germ_nodes, log_fields, reaction_rates):
    log_padded = jnp.pad(log_fields, ((0, 0), (1, 1), (1, 1)))
    first = project(modes_now, basis_rows, quad_weights, germ_nodes, log_padded, reaction_rates)
    iterate_one = (modes_now.astype(jnp.float32) + 0.04 * first).astype(jnp.bfloat16)
    second = project(iterate_one, basis_rows, quad_weights, germ_nodes, log_padded, reaction_rates)
    return modes_now.astype(jnp.float32) + 0.04 * second
```

```python
import functools

import jax
import jax.numpy as jnp
from jax import lax
from jax.experimental import pallas as pl
from jax.experimental.pallas import tpu as pltpu
from jax.sharding import PartitionSpec as P

STEP = 0.04
BF = jnp.bfloat16
F32 = jnp.float32
VM = pltpu.VMEM
OFFS = (0, -1, 1, 2)


def halo(array, axis, dim, width):
    peers, length = lax.axis_size(axis), array.shape[dim]
    up = [(i, i + 1) for i in range(peers - 1)]
    down = [(j, i) for i, j in up]
    before = lax.ppermute(lax.slice_in_dim(array, length - width, length, axis=dim), axis, up)
    after = lax.ppermute(lax.slice_in_dim(array, 0, width, axis=dim), axis, down)
    return jnp.concatenate([before, array, after], axis=dim)


def split3(x):
    hi = lax.reduce_precision(x, 8, 7)
    mid = lax.reduce_precision(x - hi, 8, 7)
    low = (x - hi) - mid
    return hi.astype(BF), mid.astype(BF), low.astype(BF)


def join3(a, b, c):
    return a.astype(F32) + (b.astype(F32) + c.astype(F32))


def ring(array, axis, stride):
    n = lax.axis_size(axis)
    fwd = [(i, (i + stride) % n) for i in range(n)]
    bwd = [(j, i) for i, j in fwd]
    below = lax.ppermute(array, axis, fwd)
    above = lax.ppermute(array, axis, bwd)
    return below, above, fwd, bwd


def gather_small(array, axis, stride):
    below, above, fwd, _ = ring(array, axis, stride)
    far = lax.ppermute(below, axis, fwd)
    return jnp.concatenate([array, below, above, far], axis=0)


def gather_large(array, axis, stride):
    below, above, fwd, bwd = ring(array, axis, stride)
    half = array.shape[0] // 2
    far0 = lax.ppermute(below[:half], axis, fwd)
    far1 = lax.ppermute(above[half:], axis, bwd)
    return [array, below, above, far0, far1]


def coef_kernel(log_ref, nodes_ref, out_ref):
    cols = [log_ref[:, j : j + 1] for j in range(8)]
    for c in range(16):
        acc = cols[0] * nodes_ref[0:1, c * 128 : (c + 1) * 128]
        for j in range(1, 8):
            acc = acc + cols[j] * nodes_ref[j : j + 1, c * 128 : (c + 1) * 128]
        out_ref[c] = jnp.exp(acc)


def drive(f_ref, h, coef_ref, c, rows, skip, rate, weight):
    def f(d):
        return f_ref[h, 20 + d : 20 + d + rows, :]

    def k(d):
        return coef_ref[c, skip + 20 + d : skip + 20 + d + rows, :]

    mid, kmid = f(0), k(0)
    total = (kmid + k(-20)) * (f(-20) - mid)
    for d in (20, -1, 1):
        total = total + (kmid + k(d)) * (f(d) - mid)
    total = total + rate * (mid - mid * mid * mid)
    return (weight * total).astype(BF)


def sweep(state, basis_refs, coef_ref, wt_ref, rate_ref, f_ref, acc_ref, rows, skip):
    acc_ref[...] = jnp.zeros_like(acc_ref)
    c = 0
    for ref in basis_refs:
        for s in range(0, ref.shape[0], 256):
            size = min(256, ref.shape[0] - s)
            block = ref[s : s + size, :]
            field = lax.dot_general(state, block, (((1,), (1,)), ((), ())), preferred_element_type=F32)
            parts = []
            for h in range(size // 128):
                f_ref[h, : field.shape[0], :] = field[:, h * 128 : (h + 1) * 128]
                parts.append(
                    drive(f_ref, h, coef_ref, c, rows, skip, rate_ref[c : c + 1, :], wt_ref[c : c + 1, :])
                )
                c += 1
            w = jnp.concatenate(parts, axis=1) if len(parts) > 1 else parts[0]
            acc_ref[...] += jnp.dot(w, block, preferred_element_type=F32)


def first_kernel(*refs):
    basis_refs = refs[:10]
    state_ref, coef_ref, wt_ref, rate_ref, out_ref, f_ref, acc_ref = refs[10:]
    sweep(state_ref[...], basis_refs, coef_ref, wt_ref, rate_ref, f_ref, acc_ref, 200, 0)
    out_ref[...] = acc_ref[...].astype(BF)


def second_kernel(*refs):
    basis_refs = refs[:10]
    state_ref, coef_ref, wt_ref, rate_ref, own_ref, other_ref, mask_ref, out_ref, f_ref, acc_ref = refs[10:]
    total = own_ref[...].astype(F32) + other_ref[...].astype(F32)
    now = state_ref[...].astype(F32)[20:220]
    state = ((now + STEP * total) * mask_ref[...][:, 0:1]).astype(BF)
    sweep(state, basis_refs, coef_ref, wt_ref, rate_ref, f_ref, acc_ref, 160, 20)
    out_ref[...] = acc_ref[...]


def body(modes_now, basis_rows, quad_weights, germ_nodes, log_fields, reaction_rates):
    quad, gy, gx = lax.axis_index("quad"), lax.axis_index("gy"), lax.axis_index("gx")
    zl, core, y, x = quad // 2, quad % 2, gy // 2, gx
    logs = split3(log_fields)
    chan = jnp.concatenate([modes_now, *logs], axis=0).transpose(1, 2, 0)
    ext = halo(halo(chan, "gx", 1, 2), "gy", 0, 2)
    logp = lax.dynamic_slice_in_dim(ext, zl * 16, 20, axis=1)[:, :, 64:88].reshape(240, 24)
    logp = join3(logp[:, 0:8], logp[:, 8:16], logp[:, 16:24])
    patch = jnp.stack([ext[:, 16 * d : 16 * d + 20, :64] for d in range(8)])
    patch = patch.reshape(8, 2, 120, 64).transpose(0, 2, 1, 3).reshape(8, 120, 128)
    patch = jnp.pad(patch, ((0, 0), (0, 8), (0, 0)))
    patch = patch.reshape(8, 8, 16, 128).transpose(0, 2, 1, 3).reshape(8, 16, 1024)
    part = lax.dynamic_slice_in_dim(basis_rows, (y * 4 + x) * 16, 16, axis=0)
    pars = jnp.concatenate([quad_weights[None], reaction_rates[None], germ_nodes.T], axis=0)
    pars = jnp.concatenate(split3(pars), axis=0)
    pars = jnp.pad(pars, ((0, 2), (0, 0))).reshape(8, 1024)
    same = jnp.concatenate([part, pars], axis=0)
    send = jnp.concatenate([patch, jnp.broadcast_to(same[None], (8, 24, 1024))], axis=1)
    groups = [list(range(0, 16, 2)), list(range(1, 16, 2))]
    recv = lax.all_to_all(send, "quad", 0, 0, axis_index_groups=groups, tiled=True)
    sub = recv[:, 16:32].reshape(8, 2, 8, 1024)
    first, second = sub[:, 0].reshape(64, 1024), sub[:, 1].reshape(64, 1024)
    a_row = gather_small(first, "gx", 1)
    b_col = gather_small(second, "gy", 2)
    blocks = gather_large(a_row, "gy", 2) + gather_large(b_col, "gx", 1)
    mine = recv[:, :16]
    swap = [(i, i ^ 1) for i in range(16)]
    theirs = lax.ppermute(mine, "quad", swap)
    pair = jnp.where(core == 0, jnp.stack([mine, theirs]), jnp.stack([theirs, mine]))
    pair = pair.reshape(2, 8, 16, 8, 2, 64).transpose(4, 3, 2, 1, 0, 5)
    state = pair.reshape(2, 128, 1024)[:, :120].reshape(240, 1024)
    pars = recv[:, 32:].reshape(8, 32, 256)[:, :30].reshape(8, 3, 10, 16, 2, 8)
    pars = join3(pars[:, 0], pars[:, 1], pars[:, 2])
    pars = pars.transpose(1, 3, 2, 0, 4).reshape(10, 2, 4, 4, 64)
    oy = jnp.asarray([d for d in OFFS], jnp.int32)
    pars = jnp.take(jnp.take(pars, (y + oy) % 4, axis=2), (x + oy) % 4, axis=3)
    pars = jnp.concatenate(
        [pars[:, 0].reshape(10, 1024), pars[:, 1].transpose(0, 2, 1, 3).reshape(10, 1024)], axis=1
    )
    wts, rates, nodes = pars[0].reshape(16, 128), pars[1].reshape(16, 128), pars[2:]
    coef = pl.pallas_call(
        coef_kernel, out_shape=jax.ShapeDtypeStruct((16, 240, 128), F32), name="coef"
    )(logp, nodes)
    part1 = pl.pallas_call(
        first_kernel,
        out_shape=jax.ShapeDtypeStruct((200, 1024), BF),
        scratch_shapes=[VM((2, 240, 128), F32), VM((200, 1024), F32)],
        name="first",
    )(*blocks, state, coef, wts, rates)
    other1 = lax.ppermute(part1, "quad", swap)
    cell = jnp.arange(200)
    row, col = gy * 8 + cell // 20 - 1, gx * 128 + zl * 16 + cell % 20 - 2
    inside = (row >= 0) & (row < 64) & (col >= 0) & (col < 512)
    mask = jnp.broadcast_to(inside.astype(F32)[:, None], (200, 128))
    part2 = pl.pallas_call(
        second_kernel,
        out_shape=jax.ShapeDtypeStruct((160, 1024), F32),
        scratch_shapes=[VM((2, 200, 128), F32), VM((160, 1024), F32)],
        name="second",
    )(*blocks, state, coef, wts, rates, part1, other1, mask)
    out = part2.astype(BF).reshape(2, 4, 20, 16, 64)[:, :, 2:18]
    out = out.transpose(3, 1, 2, 0, 4).reshape(16, 64, 128)
    back = lax.all_to_all(out, "quad", 0, 0, tiled=True)
    back = back.reshape(8, 2, 64, 128).astype(F32).sum(axis=1)
    back = back.reshape(8, 4, 16, 2, 64).transpose(4, 3, 1, 0, 2).reshape(64, 8, 128)
    return modes_now.astype(F32) + STEP * back


def solution(mesh):
    in_specs = (
        P("quad", "gy", "gx"),
        P("quad", None),
        P("quad"),
        P("quad", None),
        P(None, "gy", "gx"),
        P("quad"),
    )
    out_specs = P("quad", "gy", "gx")
    return jax.shard_map(body, mesh=mesh, in_specs=in_specs, out_specs=out_specs, check_vma=False)
```

```python
import jax
import jax.numpy as jnp
from jax import lax
from jax.experimental import pallas as pl
from jax.experimental.pallas import tpu as pltpu
from jax.sharding import PartitionSpec as P

STEP = 0.04
BF = jnp.bfloat16
F32 = jnp.float32
VM = pltpu.VMEM
OFFS = (0, -1, 1, 2)
ALL = ("quad", "gy", "gx")


def device(quad, gy, gx):
    return (quad * 8 + gy) * 4 + gx


def plane_shift(phase, step):
    pairs = []
    for quad in range(16):
        for gy in range(8):
            for gx in range(4):
                if (quad + phase) % 2 == 0:
                    to = device(quad, gy, (gx + step) % 4)
                else:
                    to = device(quad, (gy + 2 * step) % 8, gx)
                pairs.append((device(quad, gy, gx), to))
    return pairs


def shape(dims, kind):
    return jax.ShapeDtypeStruct(dims, kind)


def halves(low, high):
    lane = lax.broadcasted_iota(jnp.int32, low.shape, 1)
    return jnp.where(lane < 64, low, high)


def swapped(x):
    return pltpu.roll(x, 64, 1)


def channels_kernel(modes_ref, logs_ref, chan_ref, last_ref, lead_ref, scr_ref, log_ref):
    scr_ref[...] = modes_ref[...].astype(F32)
    log_ref[...] = logs_ref[...]
    zeros = jnp.zeros((48, 128), F32)
    for y in range(8):
        block = scr_ref[pl.ds(y, 64, stride=8), :]
        logs = log_ref[pl.ds(y, 8, stride=8), :]
        high = logs.astype(BF).astype(F32)
        turned = jnp.concatenate([block, high, logs - high, zeros], axis=0).T
        chan_ref[y] = turned
        last_ref[y * 8 : y * 8 + 8] = turned[120:128].astype(BF)
        lead_ref[y * 8 : y * 8 + 8] = turned[0:8].astype(BF)


def pack_rows(ext_ref, r, out_ref, scr_ref):
    scr_ref[...] = jnp.zeros_like(scr_ref)
    scr_ref[0:132, :] = halves(ext_ref[r, 0:132, :], swapped(ext_ref[r + 1, 0:132, :]))
    lane = lax.broadcasted_iota(jnp.int32, (33, 128), 1)
    logs = jnp.zeros((33, 128), F32)
    for g in range(4):
        for k in range(2):
            at = g * 32 + k * 16
            piece = pltpu.roll(ext_ref[r + k, g * 33 : (g + 1) * 33, :], (at - 64) % 128, 1)
            logs = jnp.where((lane >= at) & (lane < at + 16), piece, logs)
    scr_ref[136:169, :] = logs
    out_ref[...] = scr_ref[...].astype(BF)


def edges_kernel(chan_ref, left_ref, right_ref, ext_ref, low_ref, top_ref, scr_ref):
    left, right = left_ref[...].astype(F32), right_ref[...].astype(F32)
    for y in range(8):
        ext_ref[y, 0:2, :] = left[y * 8 + 6 : y * 8 + 8]
        ext_ref[y, 2:130, :] = chan_ref[y]
        ext_ref[y, 130:132, :] = right[y * 8 : y * 8 + 2]
    pack_rows(ext_ref, 6, low_ref, scr_ref)
    pack_rows(ext_ref, 0, top_ref, scr_ref)


def unpack_rows(got_ref, r, full_ref):
    got = got_ref[...].astype(F32)
    modes, logs = got[0:132], got[136:169]
    lane = lax.broadcasted_iota(jnp.int32, (33, 128), 1)
    for k in range(2):
        full_ref[r + k, 0:132, :] = modes if k == 0 else swapped(modes)
        for g in range(4):
            piece = pltpu.roll(logs, (64 - g * 32 - k * 16) % 128, 1)
            old = full_ref[r + k, g * 33 : (g + 1) * 33, :]
            full_ref[r + k, g * 33 : (g + 1) * 33, :] = jnp.where(lane < 64, old, piece)


def patches_kernel(at_ref, ext_ref, above_ref, below_ref, pars_ref, send_ref, logp_ref, full_ref, joint_ref, scr_ref):
    full_ref[2:10, 0:132, :] = ext_ref[:, 0:132, :]
    unpack_rows(above_ref, 0, full_ref)
    unpack_rows(below_ref, 10, full_ref)
    for r in range(6):
        joint_ref[r, 0:132, :] = halves(full_ref[r, 0:132, :], swapped(full_ref[r + 6, 0:132, :]))
    pars = pars_ref[...]
    high = pars.astype(BF).astype(F32)
    for d in range(8):
        for r in range(6):
            scr_ref[r * 20 : r * 20 + 20, :] = joint_ref[r, 16 * d : 16 * d + 20, :]
        scr_ref[120:140, :] = high
        scr_ref[140:160, :] = pars - high
        send_ref[d] = scr_ref[...].astype(BF)
    start = pl.multiple_of(at_ref[0] * 16, 16)
    for r in range(12):
        got = full_ref[r, pl.ds(start, 24), :]
        logp_ref[r * 20 : r * 20 + 20, :] = (got + pltpu.roll(got, 120, 1))[0:20]


def prepare_kernel(at_ref, mine_ref, theirs_ref, logp_ref, state_ref, coef_ref, wr_ref, scr_ref, par_ref):
    core = at_ref[1]
    full = jnp.zeros((8, 128), jnp.int32) + core
    for z in range(8):
        mine, theirs = mine_ref[z].astype(F32), theirs_ref[z].astype(F32)
        scr_ref[z * 160 : (z + 1) * 160, :] = mine
        flag = full[0:1, :] == 0
        zero = jnp.where(flag, mine[0:120], theirs[0:120])
        one = jnp.where(flag, theirs[0:120], mine[0:120])
        both = jnp.concatenate([halves(zero, swapped(one)), halves(swapped(zero), one)], axis=0)
        state_ref[:, z * 128 : (z + 1) * 128] = both.astype(BF)
    sub = lax.broadcasted_iota(jnp.int32, (8, 128), 0)
    grp = lax.broadcasted_iota(jnp.int32, (8, 128), 1) // 16
    for v in range(10):
        for h in range(2):
            at = 120 + v * 2 + h
            got = scr_ref[pl.ds(at, 8, stride=160), :] + scr_ref[pl.ds(at + 20, 8, stride=160), :]
            for s in (1, 2, 4):
                up = pltpu.roll(pltpu.roll(got, 8 - s, 0), 16 * s, 1)
                down = pltpu.roll(pltpu.roll(got, s, 0), 128 - 16 * s, 1)
                mine, bit = (sub & s) > 0, (grp & s) > 0
                got = jnp.where(mine == bit, got, jnp.where(mine, down, up))
            par_ref[v, h * 8 : h * 8 + 8, :] = got
    cols = [logp_ref[:, 64 + j : 65 + j] for j in range(8)]
    for n in range(16):
        p = at_ref[2 + n]
        for v in range(2):
            wr_ref[v, n : n + 1, :] = par_ref[v, pl.ds(p, 1), :]
        acc = cols[0] * par_ref[2, pl.ds(p, 1), :]
        for j in range(1, 8):
            acc = acc + cols[j] * par_ref[2 + j, pl.ds(p, 1), :]
        coef_ref[n] = jnp.exp(acc)


def drive(f_ref, h, coef_ref, c, rows, skip, rate, weight):
    def f(d):
        return f_ref[h, 20 + d : 20 + d + rows, :]

    def k(d):
        return coef_ref[c, skip + 20 + d : skip + 20 + d + rows, :]

    mid, kmid = f(0), k(0)
    total = (kmid + k(-20)) * (f(-20) - mid)
    for d in (20, -1, 1):
        total = total + (kmid + k(d)) * (f(d) - mid)
    total = total + rate * (mid - mid * mid * mid)
    return (weight * total).astype(BF)


def sweep(state, basis_refs, coef_ref, wr_ref, f_ref, acc_ref, rows, skip):
    acc_ref[...] = jnp.zeros_like(acc_ref)
    c = 0
    for ref in basis_refs:
        for s in range(0, ref.shape[0], 256):
            block = ref[s : s + 256, :]
            field = lax.dot_general(state, block, (((1,), (1,)), ((), ())), preferred_element_type=F32)
            parts = []
            for h in range(2):
                f_ref[h, : field.shape[0], :] = field[:, h * 128 : (h + 1) * 128]
                weight, rate = wr_ref[0, c : c + 1, :], wr_ref[1, c : c + 1, :]
                parts.append(drive(f_ref, h, coef_ref, c, rows, skip, rate, weight))
                c += 1
            acc_ref[...] += jnp.dot(jnp.concatenate(parts, axis=1), block, preferred_element_type=F32)


def first_kernel(b0, b1, b2, b3, b4, state_ref, coef_ref, wr_ref, out_ref, f_ref, acc_ref):
    sweep(state_ref[...], (b0, b1, b2, b3, b4), coef_ref, wr_ref, f_ref, acc_ref, 200, 0)
    out_ref[...] = acc_ref[...].astype(BF)


def second_kernel(
    edge_ref, b0, b1, b2, b3, b4, state_ref, coef_ref, wr_ref, own_ref, other_ref, out_ref, f_ref, acc_ref
):
    total = own_ref[...].astype(F32) + other_ref[...].astype(F32)
    now = state_ref[...].astype(F32)[20:220]
    cell = lax.broadcasted_iota(jnp.int32, (200, 128), 0).astype(F32)
    row = jnp.floor((cell + 0.5) * 0.05)
    col = cell - 20.0 * row
    low = jnp.where(edge_ref[0] == 1, 1.0, 0.0)
    high = jnp.where(edge_ref[1] == 1, 8.0, 9.0)
    left = jnp.where(edge_ref[2] == 1, 2.0, 0.0)
    right = jnp.where(edge_ref[3] == 1, 17.0, 19.0)
    inside = (row >= low) & (row <= high) & (col >= left) & (col <= right)
    keep = jnp.where(inside, 1.0, 0.0)[:, 0:1]
    state = ((now + STEP * total) * keep).astype(BF)
    sweep(state, (b0, b1, b2, b3, b4), coef_ref, wr_ref, f_ref, acc_ref, 160, 20)
    for z in range(8):
        for y in range(4):
            low = acc_ref[y * 20 + 2 : y * 20 + 18, z * 128 : (z + 1) * 128]
            high = acc_ref[y * 20 + 82 : y * 20 + 98, z * 128 : (z + 1) * 128]
            out_ref[2 * z, y * 16 : y * 16 + 16, :] = halves(low, swapped(high)).astype(BF)
            out_ref[2 * z + 1, y * 16 : y * 16 + 16, :] = halves(swapped(low), high).astype(BF)


def finish_kernel(back_ref, modes_ref, out_ref, scr_ref):
    for y in range(4):
        parts = [
            back_ref[2 * z, y * 16 : y * 16 + 16, :].astype(F32) + back_ref[2 * z + 1, y * 16 : y * 16 + 16, :].astype(F32)
            for z in range(8)
        ]
        turned = jnp.concatenate(parts, axis=0).T
        scr_ref[pl.ds(y, 64, stride=8), :] = turned[0:64]
        scr_ref[pl.ds(y + 4, 64, stride=8), :] = turned[64:128]
    out_ref[...] = modes_ref[...].astype(F32) + STEP * scr_ref[...]


SMEM = pl.BlockSpec(memory_space=pltpu.SMEM)
WHOLE = pl.BlockSpec(memory_space=pltpu.VMEM)


def call(kernel, outs, scratch, scalars, *args):
    specs = [SMEM] * scalars + [WHOLE] * (len(args) - scalars)
    single = not isinstance(outs, (list, tuple))
    return pl.pallas_call(
        kernel,
        out_shape=outs,
        in_specs=specs,
        out_specs=WHOLE if single else [WHOLE] * len(outs),
        scratch_shapes=scratch,
        name=kernel.__name__,
    )(*args)


def body(modes_now, basis_rows, quad_weights, germ_nodes, log_fields, reaction_rates):
    quad, gy, gx = lax.axis_index("quad"), lax.axis_index("gy"), lax.axis_index("gx")
    zl, core, y, x = quad // 2, quad % 2, gy // 2, gx
    columns = [list(range(0, 16, 2)), list(range(1, 16, 2))]
    swap = [(i, i ^ 1) for i in range(16)]

    part = lax.dynamic_slice_in_dim(basis_rows, (y * 4 + x) * 16, 16, axis=0)
    send = jnp.broadcast_to(part[None], (8, 16, 1024))
    shard = lax.all_to_all(send, "quad", 0, 0, axis_index_groups=columns, tiled=True).reshape(128, 1024)

    modes = modes_now.reshape(512, 128)
    chan, last, lead = call(
        channels_kernel,
        [shape((8, 128, 128), F32), shape((64, 128), BF), shape((64, 128), BF)],
        [VM((512, 128), F32), VM((64, 128), F32)],
        0,
        modes,
        log_fields.reshape(64, 128),
    )
    right = [(i, i + 1) for i in range(3)]
    from_left = lax.ppermute(last, "gx", right)
    from_right = lax.ppermute(lead, "gx", [(j, i) for i, j in right])
    ext, low, top = call(
        edges_kernel,
        [shape((8, 136, 128), F32), shape((176, 128), BF), shape((176, 128), BF)],
        [VM((176, 128), F32)],
        0,
        chan,
        from_left,
        from_right,
    )
    down = [(i, i + 1) for i in range(7)]
    above = lax.ppermute(low, "gy", down)
    below = lax.ppermute(top, "gy", [(j, i) for i, j in down])
    pars = jnp.concatenate([quad_weights[None], reaction_rates[None], germ_nodes.T], axis=0).reshape(20, 128)
    offs = jnp.asarray(OFFS, jnp.int32)
    outer, inner = offs[:, None], offs[None, :]
    dy, dx = jnp.where(core == 0, outer, inner), jnp.where(core == 0, inner, outer)
    order = (((y + dy) % 4) * 4 + (x + dx) % 4).reshape(16)
    at = jnp.concatenate([jnp.stack([zl, core]), order]).astype(jnp.int32)
    patch, logp = call(
        patches_kernel,
        [shape((8, 160, 128), BF), shape((240, 128), F32)],
        [VM((12, 152, 128), F32), VM((6, 136, 128), F32), VM((160, 128), F32)],
        1,
        at,
        ext,
        above,
        below,
        pars,
    )
    mine = lax.all_to_all(patch, "quad", 0, 0, axis_index_groups=columns, tiled=True)
    theirs = lax.ppermute(mine, "quad", swap)

    fwd, bwd = plane_shift(0, 1), plane_shift(0, -1)
    less = lax.ppermute(shard, ALL, fwd)
    more = lax.ppermute(shard, ALL, bwd)
    far = lax.ppermute(less, ALL, fwd)
    line = jnp.concatenate([shard, less, more, far], axis=0)
    fwd, bwd = plane_shift(1, 1), plane_shift(1, -1)
    less = lax.ppermute(line, ALL, fwd)
    more = lax.ppermute(line, ALL, bwd)
    far0 = lax.ppermute(less[:256], ALL, fwd)
    far1 = lax.ppermute(more[256:], ALL, bwd)
    blocks = (line, less, more, far0, far1)

    state, coef, wr = call(
        prepare_kernel,
        [shape((240, 1024), BF), shape((16, 240, 128), F32), shape((2, 16, 128), F32)],
        [VM((1280, 128), F32), VM((10, 16, 128), F32)],
        1,
        at,
        mine,
        theirs,
        logp,
    )
    own = call(
        first_kernel,
        shape((200, 1024), BF),
        [VM((2, 240, 128), F32), VM((200, 1024), F32)],
        0,
        *blocks,
        state,
        coef,
        wr,
    )
    other = lax.ppermute(own, "quad", swap)
    edge = jnp.stack([gy == 0, gy == 7, (gx == 0) & (zl == 0), (gx == 3) & (zl == 7)]).astype(jnp.int32)
    out = call(
        second_kernel,
        shape((16, 64, 128), BF),
        [VM((2, 200, 128), F32), VM((160, 1024), F32)],
        1,
        edge,
        *blocks,
        state,
        coef,
        wr,
        own,
        other,
    )
    back = lax.all_to_all(out, "quad", 0, 0, tiled=True)
    result = call(finish_kernel, shape((512, 128), F32), [VM((512, 128), F32)], 0, back, modes)
    return result.reshape(64, 8, 128)


def solution(mesh):
    in_specs = (
        P("quad", "gy", "gx"),
        P("quad", None),
        P("quad"),
        P("quad", None),
        P(None, "gy", "gx"),
        P("quad"),
    )
    out_specs = P("quad", "gy", "gx")
    return jax.shard_map(body, mesh=mesh, in_specs=in_specs, out_specs=out_specs, check_vma=False)
```

```python
import jax
import jax.numpy as jnp
from jax import lax
from jax.experimental import pallas as pl
from jax.experimental.pallas import tpu as pltpu
from jax.sharding import PartitionSpec as P


STEP = 0.04
BF = jnp.bfloat16
F32 = jnp.float32
VM = pltpu.VMEM
OFFS = (0, -1, 1, 2)
ARRIVAL = tuple((o, i) for o, half in ((0, 0), (0, 2), (1, 0), (2, 0), (1, 2), (2, 2), (3, 0), (3, 2)) for i in (half, half + 1))
ALL = ("quad", "gy", "gx")


def device(quad, gy, gx):
    return (quad * 8 + gy) * 4 + gx


def plane_shift(phase, step):
    pairs = []
    for quad in range(16):
        for gy in range(8):
            for gx in range(4):
                if (quad + phase) % 2 == 0:
                    to = device(quad, gy, (gx + step) % 4)
                else:
                    to = device(quad, (gy + 2 * step) % 8, gx)
                pairs.append((device(quad, gy, gx), to))
    return pairs


def shape(dims, kind):
    return jax.ShapeDtypeStruct(dims, kind)


def halves(low, high):
    lane = lax.broadcasted_iota(jnp.int32, low.shape, 1)
    return jnp.where(lane < 64, low, high)


def swapped(x):
    return pltpu.roll(x, 64, 1)


def rows_kernel(modes_ref, logs_ref, low_ref, top_ref, scr_ref, log_ref):
    scr_ref[...] = modes_ref[...].astype(F32)
    log_ref[...] = logs_ref[...]
    for out_ref, first in ((low_ref, 6), (top_ref, 0)):
        for k in range(2):
            logs = log_ref[pl.ds(first + k, 8, stride=8), :]
            high = logs.astype(BF).astype(F32)
            block = scr_ref[pl.ds(first + k, 64, stride=8), :]
            out_ref[k * 80 : k * 80 + 80, :] = jnp.concatenate([block, high, logs - high], axis=0).astype(BF)


def channels_kernel(modes_ref, logs_ref, chan_ref, scr_ref, log_ref):
    scr_ref[...] = modes_ref[...].astype(F32)
    log_ref[...] = logs_ref[...]
    zeros = jnp.zeros((48, 128), F32)
    for y in range(8):
        block = scr_ref[pl.ds(y, 64, stride=8), :]
        logs = log_ref[pl.ds(y, 8, stride=8), :]
        high = logs.astype(BF).astype(F32)
        chan_ref[y] = jnp.concatenate([block, high, logs - high, zeros], axis=0).T


def edges_kernel(chan_ref, above_ref, below_ref, full_ref, last_ref, lead_ref):
    zeros = jnp.zeros((48, 128), F32)
    for got_ref, first in ((above_ref, 0), (below_ref, 10)):
        got = got_ref[...].astype(F32)
        for k in range(2):
            full_ref[first + k, 8:136, :] = jnp.concatenate([got[k * 80 : k * 80 + 80], zeros], axis=0).T
    full_ref[2:10, 8:136, :] = chan_ref[...]
    for r in range(12):
        last_ref[r * 8 : r * 8 + 8] = full_ref[r, 128:136, :].astype(BF)
        lead_ref[r * 8 : r * 8 + 8] = full_ref[r, 8:16, :].astype(BF)


def patches_kernel(at_ref, full_ref, left_ref, right_ref, pars_ref, send_ref, logp_ref, wide_ref, joint_ref, scr_ref):
    left, right = left_ref[...].astype(F32), right_ref[...].astype(F32)
    for r in range(12):
        wide_ref[r, 0:8, :] = left[r * 8 : r * 8 + 8]
        wide_ref[r, 8:136, :] = full_ref[r, 8:136, :]
        wide_ref[r, 136:144, :] = right[r * 8 : r * 8 + 8]
    for r in range(6):
        joint_ref[r] = halves(wide_ref[r, 6:138, :], swapped(wide_ref[r + 6, 6:138, :]))
    pars = pars_ref[...]
    high = pars.astype(BF).astype(F32)
    for d in range(8):
        for r in range(6):
            scr_ref[r * 20 : r * 20 + 20, :] = joint_ref[r, 16 * d : 16 * d + 20, :]
        scr_ref[120:140, :] = high
        scr_ref[140:160, :] = pars - high
        send_ref[d] = scr_ref[...].astype(BF)
    start = pl.multiple_of(at_ref[0] * 16, 16)
    for r in range(12):
        got = wide_ref[r, pl.ds(start, 32), :]
        logp_ref[r * 20 : r * 20 + 20, :] = (got + pltpu.roll(got, 120, 1))[6:26]


def coef_kernel(at_ref, mine_ref, logp_ref, coef_ref, wr_ref, scr_ref, par_ref):
    for z in range(8):
        scr_ref[z * 40 : (z + 1) * 40, :] = mine_ref[z].astype(F32)[120:160]
    sub = lax.broadcasted_iota(jnp.int32, (8, 128), 0)
    grp = lax.broadcasted_iota(jnp.int32, (8, 128), 1) // 16
    for v in range(10):
        for h in range(2):
            at = v * 2 + h
            got = scr_ref[pl.ds(at, 8, stride=40), :] + scr_ref[pl.ds(at + 20, 8, stride=40), :]
            for s in (1, 2, 4):
                up = pltpu.roll(pltpu.roll(got, 8 - s, 0), 16 * s, 1)
                down = pltpu.roll(pltpu.roll(got, s, 0), 128 - 16 * s, 1)
                mine, bit = (sub & s) > 0, (grp & s) > 0
                got = jnp.where(mine == bit, got, jnp.where(mine, down, up))
            par_ref[v, h * 8 : h * 8 + 8, :] = got
    cols = [logp_ref[:, 64 + j : 65 + j] for j in range(8)]
    for n in range(16):
        p = at_ref[2 + n]
        for v in range(2):
            wr_ref[v, n : n + 1, :] = par_ref[v, pl.ds(p, 1), :]
        acc = cols[0] * par_ref[2, pl.ds(p, 1), :]
        for j in range(1, 8):
            acc = acc + cols[j] * par_ref[2 + j, pl.ds(p, 1), :]
        coef_ref[n] = jnp.exp(acc)


def state_kernel(at_ref, mine_ref, theirs_ref, state_ref):
    first = jnp.zeros((1, 128), jnp.int32) + at_ref[1] == 0
    for z in range(8):
        mine, theirs = mine_ref[z].astype(F32)[0:120], theirs_ref[z].astype(F32)[0:120]
        zero, one = jnp.where(first, mine, theirs), jnp.where(first, theirs, mine)
        both = jnp.concatenate([halves(zero, swapped(one)), halves(swapped(zero), one)], axis=0)
        state_ref[:, z * 128 : (z + 1) * 128] = both.astype(BF)


def drive(f_ref, h, coef_ref, c, rows, skip, rate, weight):
    def f(d):
        return f_ref[h, 20 + d : 20 + d + rows, :]

    def k(d):
        return coef_ref[c, skip + 20 + d : skip + 20 + d + rows, :]

    mid, kmid = f(0), k(0)
    total = (kmid + k(-20)) * (f(-20) - mid)
    for d in (20, -1, 1):
        total = total + (kmid + k(d)) * (f(d) - mid)
    total = total + rate * (mid - mid * mid * mid)
    return (weight * total).astype(BF)


def sweep(state, basis_refs, coef_ref, wr_ref, f_ref, acc_ref, rows, skip, c=0):
    for ref in basis_refs:
        block = ref[...]
        field = lax.dot_general(state, block, (((1,), (1,)), ((), ())), preferred_element_type=F32)
        parts = []
        for h in range(2):
            f_ref[h, : field.shape[0], :] = field[:, h * 128 : (h + 1) * 128]
            weight, rate = wr_ref[0, c : c + 1, :], wr_ref[1, c : c + 1, :]
            parts.append(drive(f_ref, h, coef_ref, c, rows, skip, rate, weight))
            c += 1
        acc_ref[...] += jnp.dot(jnp.concatenate(parts, axis=1), block, preferred_element_type=F32)


def early_kernel(b0, b1, b2, b3, state_ref, coef_ref, wr_ref, acc_ref, f_ref):
    acc_ref[...] = jnp.zeros_like(acc_ref)
    sweep(state_ref[...], (b0, b1, b2, b3), coef_ref, wr_ref, f_ref, acc_ref, 200, 0)


def late_kernel(b4, b5, b6, b7, state_ref, coef_ref, wr_ref, sum_ref, out_ref, f_ref, acc_ref):
    acc_ref[...] = sum_ref[...]
    sweep(state_ref[...], (b4, b5, b6, b7), coef_ref, wr_ref, f_ref, acc_ref, 200, 0, 8)
    out_ref[...] = acc_ref[...].astype(BF)


def second_kernel(
    edge_ref, b0, b1, b2, b3, b4, b5, b6, b7, state_ref, coef_ref, wr_ref, own_ref, other_ref, out_ref, f_ref, acc_ref
):
    total = own_ref[...].astype(F32) + other_ref[...].astype(F32)
    now = state_ref[...].astype(F32)[20:220]
    cell = lax.broadcasted_iota(jnp.int32, (200, 128), 0).astype(F32)
    row = jnp.floor((cell + 0.5) * 0.05)
    col = cell - 20.0 * row
    low = jnp.where(edge_ref[0] == 1, 1.0, 0.0)
    high = jnp.where(edge_ref[1] == 1, 8.0, 9.0)
    left = jnp.where(edge_ref[2] == 1, 2.0, 0.0)
    right = jnp.where(edge_ref[3] == 1, 17.0, 19.0)
    inside = (row >= low) & (row <= high) & (col >= left) & (col <= right)
    keep = jnp.where(inside, 1.0, 0.0)[:, 0:1]
    state = ((now + STEP * total) * keep).astype(BF)
    acc_ref[...] = jnp.zeros_like(acc_ref)
    sweep(state, (b0, b1, b2, b3, b4, b5, b6, b7), coef_ref, wr_ref, f_ref, acc_ref, 160, 20)
    for z in range(8):
        for y in range(4):
            low = acc_ref[y * 20 + 2 : y * 20 + 18, z * 128 : (z + 1) * 128]
            high = acc_ref[y * 20 + 82 : y * 20 + 98, z * 128 : (z + 1) * 128]
            out_ref[2 * z, y * 16 : y * 16 + 16, :] = halves(low, swapped(high)).astype(BF)
            out_ref[2 * z + 1, y * 16 : y * 16 + 16, :] = halves(swapped(low), high).astype(BF)


def finish_kernel(back_ref, modes_ref, out_ref, scr_ref):
    for y in range(4):
        parts = [
            back_ref[2 * z, y * 16 : y * 16 + 16, :].astype(F32) + back_ref[2 * z + 1, y * 16 : y * 16 + 16, :].astype(F32)
            for z in range(8)
        ]
        turned = jnp.concatenate(parts, axis=0).T
        scr_ref[pl.ds(y, 64, stride=8), :] = turned[0:64]
        scr_ref[pl.ds(y + 4, 64, stride=8), :] = turned[64:128]
    out_ref[...] = modes_ref[...].astype(F32) + STEP * scr_ref[...]


SMEM = pl.BlockSpec(memory_space=pltpu.SMEM)
WHOLE = pl.BlockSpec(memory_space=pltpu.VMEM)


def call(kernel, outs, scratch, scalars, *args):
    specs = [SMEM] * scalars + [WHOLE] * (len(args) - scalars)
    single = not isinstance(outs, (list, tuple))
    return pl.pallas_call(
        kernel,
        out_shape=outs,
        in_specs=specs,
        out_specs=WHOLE if single else [WHOLE] * len(outs),
        scratch_shapes=scratch,
    )(*args)


def update(modes_now, basis_rows, quad_weights, germ_nodes, log_fields, reaction_rates):
    quad, gy, gx = lax.axis_index("quad"), lax.axis_index("gy"), lax.axis_index("gx")
    zl, core, y, x = quad // 2, quad % 2, gy // 2, gx
    columns = [list(range(0, 16, 2)), list(range(1, 16, 2))]
    swap = [(i, i ^ 1) for i in range(16)]

    part = lax.dynamic_slice_in_dim(basis_rows, (y * 4 + x) * 16, 16, axis=0)
    send = jnp.broadcast_to(part[None], (8, 16, 1024))
    shard = lax.all_to_all(send, "quad", 0, 0, axis_index_groups=columns, tiled=True).reshape(128, 1024)

    modes, logs = modes_now.reshape(512, 128), log_fields.reshape(64, 128)
    scratch = [VM((512, 128), F32), VM((64, 128), F32)]
    low, top = call(rows_kernel, [shape((160, 128), BF)] * 2, scratch, 0, modes, logs)
    down, right = [(i, i + 1) for i in range(7)], [(i, i + 1) for i in range(3)]
    above = lax.ppermute(low, "gy", down)
    below = lax.ppermute(top, "gy", [(j, i) for i, j in down])
    chan = call(channels_kernel, shape((8, 128, 128), F32), scratch, 0, modes, logs)
    full, last, lead = call(
        edges_kernel,
        [shape((12, 144, 128), F32), shape((96, 128), BF), shape((96, 128), BF)],
        [],
        0,
        chan,
        above,
        below,
    )
    from_left = lax.ppermute(last, "gx", right)
    from_right = lax.ppermute(lead, "gx", [(j, i) for i, j in right])
    pars = jnp.concatenate([quad_weights[None], reaction_rates[None], germ_nodes.T], axis=0).reshape(20, 128)
    outer = jnp.asarray([OFFS[o] for o, _ in ARRIVAL], jnp.int32)
    inner = jnp.asarray([OFFS[i] for _, i in ARRIVAL], jnp.int32)
    dy, dx = jnp.where(core == 0, outer, inner), jnp.where(core == 0, inner, outer)
    order = ((y + dy) % 4) * 4 + (x + dx) % 4
    at = jnp.concatenate([jnp.stack([zl, core]), order]).astype(jnp.int32)
    patch, logp = call(
        patches_kernel,
        [shape((8, 160, 128), BF), shape((240, 128), F32)],
        [VM((12, 176, 128), F32), VM((6, 132, 128), F32), VM((160, 128), F32)],
        1,
        at,
        full,
        from_left,
        from_right,
        pars,
    )
    mine = lax.all_to_all(patch, "quad", 0, 0, axis_index_groups=columns, tiled=True)
    theirs = lax.ppermute(mine, "quad", swap)

    fwd, bwd = plane_shift(0, 1), plane_shift(0, -1)
    less = lax.ppermute(shard, ALL, fwd)
    more = lax.ppermute(shard, ALL, bwd)
    near = jnp.concatenate([shard, less], axis=0)
    far = lax.ppermute(less, ALL, fwd)
    fwd, bwd = plane_shift(1, 1), plane_shift(1, -1)
    near_less = lax.ppermute(near, ALL, fwd)
    near_more = lax.ppermute(near, ALL, bwd)
    away = jnp.concatenate([more, far], axis=0)
    away_less = lax.ppermute(away, ALL, fwd)
    away_more = lax.ppermute(away, ALL, bwd)
    near_far = lax.ppermute(near_less, ALL, fwd)
    away_far = lax.ppermute(away_more, ALL, bwd)
    blocks = (near, away, near_less, near_more, away_less, away_more, near_far, away_far)

    coef, wr = call(
        coef_kernel,
        [shape((16, 240, 128), F32), shape((2, 16, 128), F32)],
        [VM((320, 128), F32), VM((10, 16, 128), F32)],
        1,
        at,
        mine,
        logp,
    )
    state = call(state_kernel, shape((240, 1024), BF), [], 1, at, mine, theirs)
    part = call(
        early_kernel, shape((200, 1024), F32), [VM((2, 240, 128), F32)], 0, *blocks[:4], state, coef, wr
    )
    own = call(
        late_kernel,
        shape((200, 1024), BF),
        [VM((2, 240, 128), F32), VM((200, 1024), F32)],
        0,
        *blocks[4:],
        state,
        coef,
        wr,
        part,
    )
    other = lax.ppermute(own, "quad", swap)
    edge = jnp.stack([gy == 0, gy == 7, (gx == 0) & (zl == 0), (gx == 3) & (zl == 7)]).astype(jnp.int32)
    out = call(
        second_kernel,
        shape((16, 64, 128), BF),
        [VM((2, 200, 128), F32), VM((160, 1024), F32)],
        1,
        edge,
        *blocks,
        state,
        coef,
        wr,
        own,
        other,
    )
    back = lax.all_to_all(out, "quad", 0, 0, tiled=True)
    result = call(finish_kernel, shape((512, 128), F32), [VM((512, 128), F32)], 0, back, modes)
    return result.reshape(64, 8, 128)


def solution(mesh):
    in_specs = (
        P("quad", "gy", "gx"),
        P("quad", None),
        P("quad"),
        P("quad", None),
        P(None, "gy", "gx"),
        P("quad"),
    )
    out_specs = P("quad", "gy", "gx")
    return jax.shard_map(update, mesh=mesh, in_specs=in_specs, out_specs=out_specs, check_vma=False)
```

```python
import itertools

import jax
import jax.numpy as jnp
from jax import lax
from jax.experimental import pallas as pl
from jax.experimental.pallas import tpu as pltpu
from jax.sharding import Mesh
from jax.sharding import PartitionSpec as P


STEP = 0.04
BF = jnp.bfloat16
F32 = jnp.float32
VM = pltpu.VMEM
OFFS = (0, -1, 1, 2)
ARRIVAL = tuple((o, i) for o, half in ((0, 0), (0, 2), (1, 0), (2, 0), (1, 2), (2, 2), (3, 0), (3, 2)) for i in (half, half + 1))
ALL = ("zl", "core", "y", "zh", "x")
SPLIT = (8, 2, 4, 2, 4)


def shift(moves):
    every = list(itertools.product(*map(range, SPLIT)))
    number = {at: i for i, at in enumerate(every)}
    pairs = ((number[at], number.get(moves(*at))) for at in every)
    return [(i, j) for i, j in pairs if j is not None]


def plane_shift(phase, step):
    def moves(zl, core, y, zh, x):
        if (core + phase) % 2 == 0:
            return zl, core, y, zh, (x + step) % 4
        return zl, core, (y + step) % 4, zh, x

    return shift(moves)


def shape(dims, kind):
    return jax.ShapeDtypeStruct(dims, kind)


def halves(low, high):
    lane = lax.broadcasted_iota(jnp.int32, low.shape, 1)
    return jnp.where(lane < 64, low, high)


def swapped(x):
    return pltpu.roll(x, 64, 1)


def rows_kernel(at_ref, modes_ref, logs_ref, out_ref, scr_ref, log_ref):
    scr_ref[...] = modes_ref[...].astype(F32)
    log_ref[...] = logs_ref[...]
    upper = jnp.zeros((1, 128), jnp.int32) + at_ref[0] == 0
    for k in range(2):
        logs = jnp.where(upper, log_ref[pl.ds(k, 8, stride=8), :], log_ref[pl.ds(6 + k, 8, stride=8), :])
        high = logs.astype(BF).astype(F32)
        block = jnp.where(upper, scr_ref[pl.ds(k, 64, stride=8), :], scr_ref[pl.ds(6 + k, 64, stride=8), :])
        out_ref[k * 80 : k * 80 + 80, :] = jnp.concatenate([block, high, logs - high], axis=0).astype(BF)


def channels_kernel(modes_ref, logs_ref, chan_ref, scr_ref, log_ref):
    scr_ref[...] = modes_ref[...].astype(F32)
    log_ref[...] = logs_ref[...]
    zeros = jnp.zeros((48, 128), F32)
    for y in range(8):
        block = scr_ref[pl.ds(y, 64, stride=8), :]
        logs = log_ref[pl.ds(y, 8, stride=8), :]
        high = logs.astype(BF).astype(F32)
        chan_ref[y] = jnp.concatenate([block, high, logs - high, zeros], axis=0).T


def edges_kernel(at_ref, chan_ref, got_ref, full_ref, last_ref, lead_ref):
    lower = at_ref[0]
    zeros = jnp.zeros((48, 128), F32)
    got = got_ref[...].astype(F32)
    for k in range(2):
        full_ref[8 - 8 * lower + k, 8:136, :] = jnp.concatenate([got[k * 80 : k * 80 + 80], zeros], axis=0).T
    for r in range(8):
        full_ref[2 * lower + r, 8:136, :] = chan_ref[r]
    for r in range(10):
        last_ref[r * 8 : r * 8 + 8] = full_ref[r, 128:136, :].astype(BF)
        lead_ref[r * 8 : r * 8 + 8] = full_ref[r, 8:16, :].astype(BF)


def patches_kernel(at_ref, full_ref, left_ref, right_ref, pars_ref, send_ref, wide_ref, cell_ref, scr_ref):
    left, right = left_ref[...].astype(F32), right_ref[...].astype(F32)
    for r in range(10):
        wide_ref[r, 0:8, :] = left[r * 8 : r * 8 + 8]
        wide_ref[r, 8:136, :] = full_ref[r, 8:136, :]
        wide_ref[r, 136:144, :] = right[r * 8 : r * 8 + 8]
    lower = jnp.zeros((1, 128), jnp.int32) + at_ref[0] == 1
    pars = pars_ref[...]
    high = pars.astype(BF).astype(F32)
    scr_ref[60:80, :] = jnp.where(lower, pars - high, high)
    scr_ref[88:96, :] = jnp.zeros((8, 128), F32)
    lane = lax.broadcasted_iota(jnp.int32, (15, 128), 1)
    for d in range(16):
        for r in range(10):
            cell_ref[r * 12 : r * 12 + 12, :] = wide_ref[r, 8 * d + 6 : 8 * d + 18, :]
        scr_ref[0:60, :] = halves(cell_ref[0:60, :], swapped(cell_ref[60:120, :]))
        logs = jnp.zeros((15, 128), F32)
        for g in range(8):
            piece = pltpu.roll(cell_ref[g * 15 : g * 15 + 15, :], (g * 16 - 64) % 128, 1)
            logs = jnp.where((lane >= g * 16) & (lane < g * 16 + 16), piece, logs)
        scr_ref[80:95, :] = logs
        send_ref[d] = scr_ref[...].astype(BF)


PLACES = (((0, 5, 2), (5, 8, 7), (8, 10, 18)), ((0, 2, 0), (2, 5, 10), (5, 10, 13)))


def coef_kernel(at_ref, mine_ref, coef_ref, wr_ref, scr_ref, par_ref, cell_ref, log_ref):
    for z in range(16):
        scr_ref[z * 20 : (z + 1) * 20, :] = mine_ref[z].astype(F32)[60:80]
    sub = lax.broadcasted_iota(jnp.int32, (8, 128), 0)
    grp = lax.broadcasted_iota(jnp.int32, (8, 128), 1) // 16
    for v in range(10):
        for h in range(2):
            at = v * 2 + h
            got = scr_ref[pl.ds(at, 8, stride=20), :] + scr_ref[pl.ds(at + 160, 8, stride=20), :]
            for s in (1, 2, 4):
                up = pltpu.roll(pltpu.roll(got, 8 - s, 0), 16 * s, 1)
                down = pltpu.roll(pltpu.roll(got, s, 0), 128 - 16 * s, 1)
                mine, bit = (sub & s) > 0, (grp & s) > 0
                got = jnp.where(mine == bit, got, jnp.where(mine, down, up))
            par_ref[v, h * 8 : h * 8 + 8, :] = got
    for zh in range(2):
        logs = mine_ref[zh * 8].astype(F32)[80:96]
        logs = logs + pltpu.roll(logs, 120, 1)
        for g in range(8):
            cell_ref[g * 15 : g * 15 + 15, :] = pltpu.roll(logs, (128 - g * 16) % 128, 1)[0:15]
        for first, last, row in PLACES[zh]:
            log_ref[row * 12 : (row + last - first) * 12, :] = cell_ref[first * 12 : last * 12, :]
    cols = [log_ref[:, j : j + 1] for j in range(8)]
    for n in range(16):
        p = at_ref[2 + n]
        for v in range(2):
            wr_ref[v, n : n + 1, :] = par_ref[v, pl.ds(p, 1), :]
        acc = cols[0] * par_ref[2, pl.ds(p, 1), :]
        for j in range(1, 8):
            acc = acc + cols[j] * par_ref[2 + j, pl.ds(p, 1), :]
        coef_ref[n] = jnp.exp(acc)


def state_kernel(at_ref, mine_ref, theirs_ref, state_ref, scr_ref):
    first = jnp.zeros((1, 128), jnp.int32) + at_ref[1] == 0
    for z in range(8):
        for zh in range(2):
            mine, theirs = mine_ref[zh * 8 + z].astype(F32)[0:60], theirs_ref[zh * 8 + z].astype(F32)[0:60]
            zero, one = jnp.where(first, mine, theirs), jnp.where(first, theirs, mine)
            both = (halves(zero, swapped(one)), halves(swapped(zero), one))
            for lo, hi, row in PLACES[zh]:
                piece = both[lo // 5][(lo % 5) * 12 : (lo % 5 + hi - lo) * 12]
                scr_ref[row * 12 : (row + hi - lo) * 12, :] = piece
        state_ref[:, z * 128 : (z + 1) * 128] = scr_ref[...].astype(BF)


def drive(f_ref, h, coef_ref, c, rows, skip, rate, weight):
    def f(d):
        return f_ref[h, 12 + d : 12 + d + rows, :]

    def k(d):
        return coef_ref[c, skip + 12 + d : skip + 12 + d + rows, :]

    mid, kmid = f(0), k(0)
    total = (kmid + k(-12)) * (f(-12) - mid)
    for d in (12, -1, 1):
        total = total + (kmid + k(d)) * (f(d) - mid)
    total = total + rate * (mid - mid * mid * mid)
    return (weight * total).astype(BF)


def sweep(state, basis_refs, coef_ref, wr_ref, f_ref, acc_ref, rows, skip, c=0):
    for ref in basis_refs:
        block = ref[...]
        field = lax.dot_general(state, block, (((1,), (1,)), ((), ())), preferred_element_type=F32)
        parts = []
        for h in range(2):
            f_ref[h, : field.shape[0], :] = field[:, h * 128 : (h + 1) * 128]
            weight, rate = wr_ref[0, c : c + 1, :], wr_ref[1, c : c + 1, :]
            parts.append(drive(f_ref, h, coef_ref, c, rows, skip, rate, weight))
            c += 1
        acc_ref[...] += jnp.dot(jnp.concatenate(parts, axis=1), block, preferred_element_type=F32)


def first_kernel(*refs):
    blocks, (state_ref, coef_ref, wr_ref, out_ref, f_ref, acc_ref) = refs[:8], refs[8:]
    acc_ref[...] = jnp.zeros_like(acc_ref)
    sweep(state_ref[...], blocks, coef_ref, wr_ref, f_ref, acc_ref, 216, 0)
    out_ref[...] = acc_ref[...].astype(BF)


def second_kernel(edge_ref, *refs):
    blocks, (state_ref, coef_ref, wr_ref, own_ref, other_ref, out_ref, f_ref, acc_ref) = refs[:8], refs[8:]
    total = own_ref[...].astype(F32) + other_ref[...].astype(F32)
    now = state_ref[...].astype(F32)[12:228]
    cell = lax.broadcasted_iota(jnp.int32, (216, 128), 0).astype(F32)
    row = jnp.floor((cell + 0.5) * (1.0 / 12.0))
    col = cell - 12.0 * row
    low = jnp.where(edge_ref[0] == 1, 1.0, 0.0)
    high = jnp.where(edge_ref[1] == 1, 16.0, 17.0)
    left = jnp.where(edge_ref[2] == 1, 2.0, 0.0)
    right = jnp.where(edge_ref[3] == 1, 9.0, 11.0)
    inside = (row >= low) & (row <= high) & (col >= left) & (col <= right)
    keep = jnp.where(inside, 1.0, 0.0)[:, 0:1]
    state = ((now + STEP * total) * keep).astype(BF)
    acc_ref[...] = jnp.zeros_like(acc_ref)
    sweep(state, blocks, coef_ref, wr_ref, f_ref, acc_ref, 192, 12)
    for zh in range(2):
        for z in range(8):
            to = (zh * 8 + z) * 2
            for y in range(4):
                at = (zh * 8 + y) * 12 + 2
                low = acc_ref[at : at + 8, z * 128 : (z + 1) * 128]
                high = acc_ref[at + 48 : at + 56, z * 128 : (z + 1) * 128]
                out_ref[to, y * 8 : y * 8 + 8, :] = halves(low, swapped(high)).astype(BF)
                out_ref[to + 1, y * 8 : y * 8 + 8, :] = halves(swapped(low), high).astype(BF)


def finish_kernel(back_ref, modes_ref, out_ref, scr_ref):
    for y in range(4):
        parts = [
            back_ref[2 * d, y * 8 : y * 8 + 8, :].astype(F32) + back_ref[2 * d + 1, y * 8 : y * 8 + 8, :].astype(F32)
            for d in range(16)
        ]
        turned = jnp.concatenate(parts, axis=0).T
        scr_ref[pl.ds(y, 64, stride=8), :] = turned[0:64]
        scr_ref[pl.ds(y + 4, 64, stride=8), :] = turned[64:128]
    out_ref[...] = modes_ref[...].astype(F32) + STEP * scr_ref[...]


SMEM = pl.BlockSpec(memory_space=pltpu.SMEM)
WHOLE = pl.BlockSpec(memory_space=pltpu.VMEM)


def call(kernel, outs, scratch, scalars, *args):
    specs = [SMEM] * scalars + [WHOLE] * (len(args) - scalars)
    single = not isinstance(outs, (list, tuple))
    return pl.pallas_call(
        kernel,
        out_shape=outs,
        in_specs=specs,
        out_specs=WHOLE if single else [WHOLE] * len(outs),
        scratch_shapes=scratch,
    )(*args)


def update(modes_now, basis_rows, quad_weights, germ_nodes, log_fields, reaction_rates):
    zl, core, y, zh, x = (lax.axis_index(axis) for axis in ALL)
    outer = jnp.asarray([OFFS[o] for o, _ in ARRIVAL], jnp.int32)
    inner = jnp.asarray([OFFS[i] for _, i in ARRIVAL], jnp.int32)
    dy, dx = jnp.where(core == 0, outer, inner), jnp.where(core == 0, inner, outer)
    order = ((y + dy) % 4) * 4 + (x + dx) % 4
    at = jnp.concatenate([jnp.stack([zh, core]), order]).astype(jnp.int32)

    part = lax.dynamic_slice_in_dim(basis_rows, (y * 4 + x) * 16, 16, axis=0)
    send = jnp.broadcast_to(part[None], (8, 16, 1024))
    shard = lax.all_to_all(send, "zl", 0, 0, tiled=True).reshape(128, 1024)

    modes, logs = modes_now.reshape(512, 128), log_fields.reshape(64, 128)
    scratch = [VM((512, 128), F32), VM((64, 128), F32)]
    rows = call(rows_kernel, shape((160, 128), BF), scratch, 1, at, modes, logs)

    def toward(zl, core, y, zh, x):
        return zl, core, y + 2 * zh - 1, zh, x

    got = lax.ppermute(rows, ALL, shift(toward))
    chan = call(channels_kernel, shape((8, 128, 128), F32), scratch, 0, modes, logs)
    full, last, lead = call(
        edges_kernel,
        [shape((10, 144, 128), F32), shape((80, 128), BF), shape((80, 128), BF)],
        [],
        1,
        at,
        chan,
        got,
    )
    right = [(i, i + 1) for i in range(3)]
    from_left = lax.ppermute(last, "x", right)
    from_right = lax.ppermute(lead, "x", [(j, i) for i, j in right])
    pars = jnp.concatenate([quad_weights[None], reaction_rates[None], germ_nodes.T], axis=0).reshape(20, 128)
    patch = call(
        patches_kernel,
        shape((16, 96, 128), BF),
        [VM((10, 144, 128), F32), VM((120, 128), F32), VM((96, 128), F32)],
        1,
        at,
        full,
        from_left,
        from_right,
        pars,
    )
    mine = lax.all_to_all(patch, ("zh", "zl"), 0, 0, tiled=True)
    theirs = lax.ppermute(mine, "core", [(0, 1), (1, 0)])

    fwd, bwd = plane_shift(0, 1), plane_shift(0, -1)
    less = lax.ppermute(shard, ALL, fwd)
    more = lax.ppermute(shard, ALL, bwd)
    near = jnp.concatenate([shard, less], axis=0)
    far = lax.ppermute(less, ALL, fwd)
    fwd, bwd = plane_shift(1, 1), plane_shift(1, -1)
    near_less = lax.ppermute(near, ALL, fwd)
    near_more = lax.ppermute(near, ALL, bwd)
    away = jnp.concatenate([more, far], axis=0)
    away_less = lax.ppermute(away, ALL, fwd)
    away_more = lax.ppermute(away, ALL, bwd)
    near_far = lax.ppermute(near_less, ALL, fwd)
    away_far = lax.ppermute(away_more, ALL, bwd)
    blocks = (near, away, near_less, near_more, away_less, away_more, near_far, away_far)

    coef, wr = call(
        coef_kernel,
        [shape((16, 240, 128), F32), shape((2, 16, 128), F32)],
        [VM((320, 128), F32), VM((10, 16, 128), F32), VM((120, 128), F32), VM((240, 128), F32)],
        1,
        at,
        mine,
    )
    state = call(state_kernel, shape((240, 1024), BF), [VM((240, 128), F32)], 1, at, mine, theirs)
    own = call(
        first_kernel,
        shape((216, 1024), BF),
        [VM((2, 240, 128), F32), VM((216, 1024), F32)],
        0,
        *blocks,
        state,
        coef,
        wr,
    )
    other = lax.ppermute(own, "core", [(0, 1), (1, 0)])
    strip = zh * 8 + zl
    edge = jnp.stack([y == 0, y == 3, (x == 0) & (strip == 0), (x == 3) & (strip == 15)]).astype(jnp.int32)
    out = call(
        second_kernel,
        shape((32, 32, 128), BF),
        [VM((2, 216, 128), F32), VM((192, 1024), F32)],
        1,
        edge,
        *blocks,
        state,
        coef,
        wr,
        own,
        other,
    )
    back = lax.all_to_all(out, ("zh", "zl", "core"), 0, 0, tiled=True)
    result = call(finish_kernel, shape((512, 128), F32), [VM((512, 128), F32)], 0, back, modes)
    return result.reshape(64, 8, 128)


def solution(mesh):
    fine = Mesh(mesh.devices.reshape(SPLIT), ALL)
    quad = ("zl", "core")
    in_specs = (P(quad, ("y", "zh"), "x"), P(quad, None), P(quad), P(quad, None), P(None, ("y", "zh"), "x"), P(quad))
    out_specs = P(quad, ("y", "zh"), "x")
    return jax.shard_map(update, mesh=fine, in_specs=in_specs, out_specs=out_specs, check_vma=False)
```

```python
import itertools

import jax
import jax.numpy as jnp
from jax import lax
from jax.experimental import pallas as pl
from jax.experimental.pallas import tpu as pltpu
from jax.sharding import Mesh
from jax.sharding import PartitionSpec as P


STEP = 0.04
BF = jnp.bfloat16
F32 = jnp.float32
VM = pltpu.VMEM
OFFS = (0, -1, 1, 2)
ARRIVAL = tuple((o, i) for o, half in ((0, 0), (0, 2), (1, 0), (2, 0), (1, 2), (2, 2), (3, 0), (3, 2)) for i in (half, half + 1))
ALL = ("zl", "core", "y", "zh", "x")
SPLIT = (8, 2, 4, 2, 4)


def shift(moves):
    every = list(itertools.product(*map(range, SPLIT)))
    number = {at: i for i, at in enumerate(every)}
    pairs = ((number[at], number.get(moves(*at))) for at in every)
    return [(i, j) for i, j in pairs if j is not None]


def plane_shift(phase, step):
    def moves(zl, core, y, zh, x):
        if (core + phase) % 2 == 0:
            return zl, core, y, zh, (x + step) % 4
        return zl, core, (y + step) % 4, zh, x

    return shift(moves)


def shape(dims, kind):
    return jax.ShapeDtypeStruct(dims, kind)


def halves(low, high):
    lane = lax.broadcasted_iota(jnp.int32, low.shape, 1)
    return jnp.where(lane < 64, low, high)


def swapped(x):
    return pltpu.roll(x, 64, 1)


def rows_kernel(modes_ref, logs_ref, out_ref, scr_ref, log_ref):
    scr_ref[...] = modes_ref[...].astype(F32)
    log_ref[...] = logs_ref[...]
    upper = jnp.zeros((1, 128), jnp.int32) + lax.axis_index("zh") == 0
    for k in range(2):
        logs = jnp.where(upper, log_ref[pl.ds(k, 8, stride=8), :], log_ref[pl.ds(6 + k, 8, stride=8), :])
        high = logs.astype(BF).astype(F32)
        block = jnp.where(upper, scr_ref[pl.ds(k, 64, stride=8), :], scr_ref[pl.ds(6 + k, 64, stride=8), :])
        out_ref[k * 80 : k * 80 + 80, :] = jnp.concatenate([block, high, logs - high], axis=0).astype(BF)


def channels_kernel(modes_ref, logs_ref, chan_ref, scr_ref, log_ref):
    scr_ref[...] = modes_ref[...].astype(F32)
    log_ref[...] = logs_ref[...]
    zeros = jnp.zeros((48, 128), F32)
    for y in range(8):
        block = scr_ref[pl.ds(y, 64, stride=8), :]
        logs = log_ref[pl.ds(y, 8, stride=8), :]
        high = logs.astype(BF).astype(F32)
        chan_ref[y] = jnp.concatenate([block, high, logs - high, zeros], axis=0).T


def edges_kernel(chan_ref, got_ref, full_ref, last_ref, lead_ref):
    lower = lax.axis_index("zh")
    zeros = jnp.zeros((48, 128), F32)
    got = got_ref[...].astype(F32)
    for k in range(2):
        full_ref[8 - 8 * lower + k, 8:136, :] = jnp.concatenate([got[k * 80 : k * 80 + 80], zeros], axis=0).T
    for r in range(8):
        full_ref[2 * lower + r, 8:136, :] = chan_ref[r]
    for r in range(10):
        last_ref[r * 8 : r * 8 + 8] = full_ref[r, 128:136, :].astype(BF)
        lead_ref[r * 8 : r * 8 + 8] = full_ref[r, 8:16, :].astype(BF)


def log_rows(cell_ref, rows):
    lane = lax.broadcasted_iota(jnp.int32, (rows, 128), 1)
    logs = jnp.zeros((rows, 128), F32)
    for g in range(8):
        piece = pltpu.roll(cell_ref[g * rows : (g + 1) * rows, :], (g * 16 - 64) % 128, 1)
        logs = jnp.where((lane >= g * 16) & (lane < g * 16 + 16), piece, logs)
    return logs


def patches_kernel(full_ref, left_ref, right_ref, pars_ref, send_ref, wide_ref, cell_ref, scr_ref):
    left, right = left_ref[...].astype(F32), right_ref[...].astype(F32)
    for r in range(10):
        wide_ref[r, 0:8, :] = left[r * 8 : r * 8 + 8]
        wide_ref[r, 8:136, :] = full_ref[r, 8:136, :]
        wide_ref[r, 136:144, :] = right[r * 8 : r * 8 + 8]
    zh = lax.axis_index("zh")
    scr_ref[...] = jnp.zeros_like(scr_ref)
    for d in range(8):
        for r in range(8):
            cell_ref[r * 20 : r * 20 + 20, :] = wide_ref[2 * zh + r, 16 * d + 6 : 16 * d + 26, :]
        scr_ref[0:80, :] = halves(cell_ref[0:80, :], swapped(cell_ref[80:160, :]))
        scr_ref[80:100, :] = log_rows(cell_ref, 20)
        send_ref[zh * 8 + d] = scr_ref[...].astype(BF)
    pars = pars_ref[...]
    high = pars.astype(BF).astype(F32)
    scr_ref[56:76, :] = high
    scr_ref[76:96, :] = pars - high
    for d in range(8):
        for r in range(4):
            cell_ref[r * 20 : r * 20 + 20, :] = wide_ref[6 - 6 * zh + r, 16 * d + 6 : 16 * d + 26, :]
        scr_ref[0:40, :] = halves(cell_ref[0:40, :], swapped(cell_ref[40:80, :]))
        scr_ref[40:50, :] = log_rows(cell_ref, 10)
        send_ref[8 - 8 * zh + d] = scr_ref[...].astype(BF)


def parameters(mine_ref, raw_ref, par_ref):
    zh = lax.axis_index("zh")
    for z in range(8):
        raw_ref[z * 40 : (z + 1) * 40, :] = mine_ref[8 - 8 * zh + z].astype(F32)[56:96]
    sub = lax.broadcasted_iota(jnp.int32, (8, 128), 0)
    grp = lax.broadcasted_iota(jnp.int32, (8, 128), 1) // 16
    for v in range(40):
        got = raw_ref[pl.ds(v, 8, stride=40), :]
        for s in (1, 2, 4):
            up = pltpu.roll(pltpu.roll(got, 8 - s, 0), 16 * s, 1)
            down = pltpu.roll(pltpu.roll(got, s, 0), 128 - 16 * s, 1)
            mine, bit = (sub & s) > 0, (grp & s) > 0
            got = jnp.where(mine == bit, got, jnp.where(mine, down, up))
        par_ref[v * 8 : v * 8 + 8, :] = got


def log_patch(mine_ref, log_ref):
    zh = lax.axis_index("zh")
    same, other = mine_ref[zh * 8].astype(F32), mine_ref[8 - 8 * zh].astype(F32)
    for g in range(8):
        log_ref[40 + g * 20 : 60 + g * 20, :] = pltpu.roll(same, (128 - g * 16) % 128, 1)[80:100]
        at = g * 10 if g < 4 else 160 + g * 10
        log_ref[at : at + 10, :] = pltpu.roll(other, (128 - g * 16) % 128, 1)[40:50]
    logs = log_ref[...]
    lane = lax.broadcasted_iota(jnp.int32, logs.shape, 1)
    return jnp.where(lane < 16, logs, pltpu.roll(logs, 16, 1))[:, 0:32].astype(BF)


def make_state(mine_ref, theirs_ref, state_ref, scr_ref):
    first = jnp.zeros((1, 128), jnp.int32) + lax.axis_index("core") == 0
    zh = lax.axis_index("zh")
    for z in range(8):
        for at, rows, lo, hi in ((zh * 8 + z, 80, 40, 120), (8 - 8 * zh + z, 40, 0, 200)):
            mine, theirs = mine_ref[at].astype(F32)[0:rows], theirs_ref[at].astype(F32)[0:rows]
            zero, one = jnp.where(first, mine, theirs), jnp.where(first, theirs, mine)
            scr_ref[lo : lo + rows, :] = halves(zero, swapped(one))
            scr_ref[hi : hi + rows, :] = halves(swapped(zero), one)
        state_ref[:, z * 128 : (z + 1) * 128] = scr_ref[...].astype(BF)


def drive(f_ref, h, coef_ref, c, rows, skip, rate, weight):
    def f(d):
        return f_ref[h, 20 + d : 20 + d + rows, :]

    def k(d):
        return coef_ref[c, skip + 20 + d : skip + 20 + d + rows, :]

    mid, kmid = f(0), k(0)
    total = (kmid + k(-20)) * (f(-20) - mid)
    for d in (20, -1, 1):
        total = total + (kmid + k(d)) * (f(d) - mid)
    total = total + rate * (mid - mid * mid * mid)
    return (weight * total).astype(BF)


def project(state, block, s, coef_ref, wr_ref, f_ref, acc_ref, rows, skip):
    field = lax.dot_general(state, block, (((1,), (1,)), ((), ())), preferred_element_type=F32)
    parts = []
    for h in range(2):
        c = s * 2 + h
        f_ref[h, : field.shape[0], :] = field[:, h * 128 : (h + 1) * 128]
        weight, rate = wr_ref[0, c : c + 1, :], wr_ref[1, c : c + 1, :]
        parts.append(drive(f_ref, h, coef_ref, c, rows, skip, rate, weight))
    part = jnp.dot(jnp.concatenate(parts, axis=1), block, preferred_element_type=F32)
    if s == 0:
        acc_ref[...] = part
    else:
        acc_ref[...] += part


def first_kernel(*refs):
    blocks, (mine_ref, theirs_ref, own_ref, state_ref, coef_ref, wr_ref) = refs[:8], refs[8:14]
    basis_ref, held_ref, f_ref, acc_ref, scr_ref, raw_ref, par_ref, log_ref, in_sem, out_sem = refs[14:]
    loads = [pltpu.make_async_copy(blocks[s], basis_ref.at[s], in_sem.at[s]) for s in range(8)]
    for load in loads:
        load.start()
    core, y, x = (lax.axis_index(axis) for axis in ("core", "y", "x"))
    parameters(mine_ref, raw_ref, par_ref)
    logs = log_patch(mine_ref, log_ref)
    make_state(mine_ref, theirs_ref, state_ref, scr_ref)
    state = state_ref[...]
    stores = []
    for s in range(8):
        nodes = []
        for h in range(2):
            o, i = ARRIVAL[s * 2 + h]
            dy, dx = jnp.where(core == 0, OFFS[o], OFFS[i]), jnp.where(core == 0, OFFS[i], OFFS[o])
            p = ((y + dy) & 3) * 4 + ((x + dx) & 3)
            for v in range(2):
                pair = par_ref[pl.ds(v * 16 + p, 1), :] + par_ref[pl.ds(160 + v * 16 + p, 1), :]
                wr_ref[v, s * 2 + h : s * 2 + h + 1, :] = pair
            high = par_ref[pl.ds(32 + p, 8, stride=16), :]
            low = par_ref[pl.ds(192 + p, 8, stride=16), :]
            nodes.append(jnp.concatenate([high, high, low, low], axis=0).astype(BF))
        power = jnp.dot(logs, jnp.concatenate(nodes, axis=1), preferred_element_type=F32)
        for h in range(2):
            held_ref[s * 2 + h] = jnp.exp(power[:, h * 128 : (h + 1) * 128])
        at = pl.ds(s * 2, 2)
        stores.append(pltpu.make_async_copy(held_ref.at[at], coef_ref.at[at], out_sem.at[s]))
        stores[-1].start()
        loads[s].wait()
        project(state, basis_ref[s], s, held_ref, wr_ref, f_ref, acc_ref, 200, 0)
    own_ref[...] = acc_ref[...].astype(BF)
    for store in stores:
        store.wait()


def second_kernel(*refs):
    blocks, (coef_ref, state_ref, wr_ref, own_ref, other_ref, out_ref) = refs[:8], refs[8:14]
    basis_ref, held_ref, f_ref, acc_ref, in_sem, coef_sem = refs[14:]
    loads = []
    for s in range(8):
        at = pl.ds(s * 2, 2)
        loads.append(pltpu.make_async_copy(blocks[s], basis_ref.at[s], in_sem.at[s]))
        loads.append(pltpu.make_async_copy(coef_ref.at[at], held_ref.at[at], coef_sem.at[s]))
    for load in loads:
        load.start()
    total = own_ref[...].astype(F32) + other_ref[...].astype(F32)
    now = state_ref[...].astype(F32)[20:220]
    cell = lax.broadcasted_iota(jnp.int32, (200, 128), 0).astype(F32)
    row = jnp.floor((cell + 0.5) * 0.05)
    col = cell - 20.0 * row
    zl, _, y, zh, x = (lax.axis_index(axis) for axis in ALL)
    low = jnp.where((y == 0) & (zh == 0), 1.0, 0.0)
    high = jnp.where((y == 3) & (zh == 1), 8.0, 9.0)
    left = jnp.where((x == 0) & (zl == 0), 2.0, 0.0)
    right = jnp.where((x == 3) & (zl == 7), 17.0, 19.0)
    inside = (row >= low) & (row <= high) & (col >= left) & (col <= right)
    keep = jnp.where(inside, 1.0, 0.0)[:, 0:1]
    state = ((now + STEP * total) * keep).astype(BF)
    for s in range(8):
        loads[2 * s].wait()
        loads[2 * s + 1].wait()
        project(state, basis_ref[s], s, held_ref, wr_ref, f_ref, acc_ref, 160, 20)
    for z in range(8):
        for y in range(4):
            low = acc_ref[y * 20 + 2 : y * 20 + 18, z * 128 : (z + 1) * 128]
            high = acc_ref[y * 20 + 82 : y * 20 + 98, z * 128 : (z + 1) * 128]
            out_ref[2 * z, y * 16 : y * 16 + 16, :] = halves(low, swapped(high)).astype(BF)
            out_ref[2 * z + 1, y * 16 : y * 16 + 16, :] = halves(swapped(low), high).astype(BF)


def finish_kernel(back_ref, modes_ref, out_ref, scr_ref):
    for y in range(4):
        parts = [
            back_ref[2 * z, y * 16 : y * 16 + 16, :].astype(F32) + back_ref[2 * z + 1, y * 16 : y * 16 + 16, :].astype(F32)
            for z in range(8)
        ]
        turned = jnp.concatenate(parts, axis=0).T
        scr_ref[pl.ds(y, 64, stride=8), :] = turned[0:64]
        scr_ref[pl.ds(y + 4, 64, stride=8), :] = turned[64:128]
    out_ref[...] = modes_ref[...].astype(F32) + STEP * scr_ref[...]


STAY = pl.BlockSpec(memory_space=pl.ANY)
WHOLE = pl.BlockSpec(memory_space=pltpu.VMEM)


def call(kernel, outs, scratch, *args, left=0, wide=()):
    single = not isinstance(outs, (list, tuple))
    specs = [STAY if i in wide else WHOLE for i in range(1 if single else len(outs))]
    return pl.pallas_call(
        kernel,
        out_shape=outs,
        in_specs=[STAY] * left + [WHOLE] * (len(args) - left),
        out_specs=specs[0] if single else specs,
        scratch_shapes=scratch,
    )(*args)


def update(modes_now, basis_rows, quad_weights, germ_nodes, log_fields, reaction_rates):
    y, x = lax.axis_index("y"), lax.axis_index("x")

    part = lax.dynamic_slice_in_dim(basis_rows, (y * 4 + x) * 16, 16, axis=0)
    send = jnp.broadcast_to(part[None], (8, 16, 1024))
    shard = lax.all_to_all(send, "zl", 0, 0, tiled=True).reshape(128, 1024)

    modes, logs = modes_now.reshape(512, 128), log_fields.reshape(64, 128)
    scratch = [VM((512, 128), F32), VM((64, 128), F32)]
    rows = call(rows_kernel, shape((160, 128), BF), scratch, modes, logs)

    def toward(zl, core, y, zh, x):
        return zl, core, y + 2 * zh - 1, zh, x

    got = lax.ppermute(rows, ALL, shift(toward))
    chan = call(channels_kernel, shape((8, 128, 128), F32), scratch, modes, logs)
    full, last, lead = call(
        edges_kernel,
        [shape((10, 144, 128), F32), shape((80, 128), BF), shape((80, 128), BF)],
        [],
        chan,
        got,
    )
    right = [(i, i + 1) for i in range(3)]
    from_left = lax.ppermute(last, "x", right)
    from_right = lax.ppermute(lead, "x", [(j, i) for i, j in right])
    pars = jnp.concatenate([quad_weights[None], reaction_rates[None], germ_nodes.T], axis=0).reshape(20, 128)
    patch = call(
        patches_kernel,
        shape((16, 104, 128), BF),
        [VM((10, 144, 128), F32), VM((160, 128), F32), VM((104, 128), F32)],
        full,
        from_left,
        from_right,
        pars,
    )
    mine = lax.all_to_all(patch, ("zh", "zl"), 0, 0, tiled=True)
    theirs = lax.ppermute(mine, "core", [(0, 1), (1, 0)])

    fwd, bwd = plane_shift(0, 1), plane_shift(0, -1)
    less = lax.ppermute(shard, ALL, fwd)
    more = lax.ppermute(shard, ALL, bwd)
    near = jnp.concatenate([shard, less], axis=0)
    far = lax.ppermute(less, ALL, fwd)
    fwd, bwd = plane_shift(1, 1), plane_shift(1, -1)
    near_less = lax.ppermute(near, ALL, fwd)
    near_more = lax.ppermute(near, ALL, bwd)
    away = jnp.concatenate([more, far], axis=0)
    away_more = lax.ppermute(away, ALL, bwd)
    away_less = lax.ppermute(away, ALL, fwd)
    near_far = lax.ppermute(near_less, ALL, fwd)
    away_far = lax.ppermute(away_more, ALL, bwd)
    blocks = (near, away, near_less, near_more, away_less, away_more, near_far, away_far)

    dma = pltpu.SemaphoreType.DMA
    held = [VM((8, 256, 1024), BF), VM((16, 240, 128), F32)]
    own, state, coef, wr = call(
        first_kernel,
        [shape((200, 1024), BF), shape((240, 1024), BF), shape((16, 240, 128), F32), shape((2, 16, 128), F32)],
        held
        + [VM((2, 240, 128), F32), VM((200, 1024), F32), VM((240, 128), F32)]
        + [VM((320, 128), F32), VM((320, 128), F32), VM((240, 128), F32), dma((8,)), dma((8,))],
        *blocks,
        mine,
        theirs,
        left=8,
        wide=(2,),
    )
    other = lax.ppermute(own, "core", [(0, 1), (1, 0)])
    out = call(
        second_kernel,
        shape((16, 64, 128), BF),
        held + [VM((2, 200, 128), F32), VM((160, 1024), F32), dma((8,)), dma((8,))],
        *blocks,
        coef,
        state,
        wr,
        own,
        other,
        left=9,
    )
    back = lax.all_to_all(out, ("zl", "core"), 0, 0, tiled=True)
    result = call(finish_kernel, shape((512, 128), F32), [VM((512, 128), F32)], back, modes)
    return result.reshape(64, 8, 128)


def solution(mesh):
    fine = Mesh(mesh.devices.reshape(SPLIT), ALL)
    quad = ("zl", "core")
    in_specs = (P(quad, ("y", "zh"), "x"), P(quad, None), P(quad), P(quad, None), P(None, ("y", "zh"), "x"), P(quad))
    out_specs = P(quad, ("y", "zh"), "x")
    return jax.shard_map(update, mesh=fine, in_specs=in_specs, out_specs=out_specs, check_vma=False)
```

```python
import itertools

import jax
import jax.numpy as jnp
from jax import lax
from jax.experimental import pallas as pl
from jax.experimental.pallas import tpu as pltpu
from jax.sharding import Mesh
from jax.sharding import PartitionSpec as P


STEP = 0.04
BF = jnp.bfloat16
F32 = jnp.float32
VM = pltpu.VMEM
OFFS = (0, -1, 1, 2)
ARRIVAL = tuple((o, i) for o, half in ((0, 0), (0, 2), (1, 0), (2, 0), (1, 2), (2, 2), (3, 0), (3, 2)) for i in (half, half + 1))
ALL = ("zl", "core", "y", "zh", "x")
SPLIT = (8, 2, 4, 2, 4)


def shift(moves):
    every = list(itertools.product(*map(range, SPLIT)))
    number = {at: i for i, at in enumerate(every)}
    pairs = ((number[at], number.get(moves(*at))) for at in every)
    return [(i, j) for i, j in pairs if j is not None]


def plane_shift(phase, step):
    def moves(zl, core, y, zh, x):
        if (core + phase) % 2 == 0:
            return zl, core, y, zh, (x + step) % 4
        return zl, core, (y + step) % 4, zh, x

    return shift(moves)


def shape(dims, kind):
    return jax.ShapeDtypeStruct(dims, kind)


def halves(low, high):
    lane = lax.broadcasted_iota(jnp.int32, low.shape, 1)
    return jnp.where(lane < 64, low, high)


def swapped(x):
    return pltpu.roll(x, 64, 1)


def rows_kernel(modes_ref, logs_ref, out_ref, scr_ref, log_ref):
    scr_ref[...] = modes_ref[...].astype(F32)
    log_ref[...] = logs_ref[...]
    upper = jnp.zeros((1, 128), jnp.int32) + lax.axis_index("zh") == 0
    for k in range(2):
        logs = jnp.where(upper, log_ref[pl.ds(k, 8, stride=8), :], log_ref[pl.ds(6 + k, 8, stride=8), :])
        high = logs.astype(BF).astype(F32)
        block = jnp.where(upper, scr_ref[pl.ds(k, 64, stride=8), :], scr_ref[pl.ds(6 + k, 64, stride=8), :])
        out_ref[k * 80 : k * 80 + 80, :] = jnp.concatenate([block, high, logs - high], axis=0).astype(BF)


def channels_kernel(modes_ref, logs_ref, chan_ref, scr_ref, log_ref):
    scr_ref[...] = modes_ref[...].astype(F32)
    log_ref[...] = logs_ref[...]
    zeros = jnp.zeros((48, 128), F32)
    for y in range(8):
        block = scr_ref[pl.ds(y, 64, stride=8), :]
        logs = log_ref[pl.ds(y, 8, stride=8), :]
        high = logs.astype(BF).astype(F32)
        chan_ref[y] = jnp.concatenate([block, high, logs - high, zeros], axis=0).T


def edges_kernel(chan_ref, got_ref, full_ref, last_ref, lead_ref):
    lower = lax.axis_index("zh")
    zeros = jnp.zeros((48, 128), F32)
    got = got_ref[...].astype(F32)
    for k in range(2):
        full_ref[8 - 8 * lower + k, 8:136, :] = jnp.concatenate([got[k * 80 : k * 80 + 80], zeros], axis=0).T
    for r in range(8):
        full_ref[2 * lower + r, 8:136, :] = chan_ref[r]
    for r in range(10):
        last_ref[r * 8 : r * 8 + 8] = full_ref[r, 128:136, :].astype(BF)
        lead_ref[r * 8 : r * 8 + 8] = full_ref[r, 8:16, :].astype(BF)


def log_rows(cell_ref, rows):
    lane = lax.broadcasted_iota(jnp.int32, (rows, 128), 1)
    logs = jnp.zeros((rows, 128), F32)
    for g in range(8):
        piece = pltpu.roll(cell_ref[g * rows : (g + 1) * rows, :], (g * 16 - 64) % 128, 1)
        logs = jnp.where((lane >= g * 16) & (lane < g * 16 + 16), piece, logs)
    return logs


def patches_kernel(full_ref, left_ref, right_ref, pars_ref, send_ref, wide_ref, cell_ref, scr_ref):
    left, right = left_ref[...].astype(F32), right_ref[...].astype(F32)
    for r in range(10):
        wide_ref[r, 0:8, :] = left[r * 8 : r * 8 + 8]
        wide_ref[r, 8:136, :] = full_ref[r, 8:136, :]
        wide_ref[r, 136:144, :] = right[r * 8 : r * 8 + 8]
    zh = lax.axis_index("zh")
    scr_ref[...] = jnp.zeros_like(scr_ref)
    for d in range(8):
        for r in range(8):
            cell_ref[r * 20 : r * 20 + 20, :] = wide_ref[2 * zh + r, 16 * d + 6 : 16 * d + 26, :]
        scr_ref[0:80, :] = halves(cell_ref[0:80, :], swapped(cell_ref[80:160, :]))
        scr_ref[80:100, :] = log_rows(cell_ref, 20)
        send_ref[zh * 8 + d] = scr_ref[...].astype(BF)
    pars = pars_ref[...]
    high = pars.astype(BF).astype(F32)
    scr_ref[56:76, :] = high
    scr_ref[76:96, :] = pars - high
    for d in range(8):
        for r in range(4):
            cell_ref[r * 20 : r * 20 + 20, :] = wide_ref[6 - 6 * zh + r, 16 * d + 6 : 16 * d + 26, :]
        scr_ref[0:40, :] = halves(cell_ref[0:40, :], swapped(cell_ref[40:80, :]))
        scr_ref[40:50, :] = log_rows(cell_ref, 10)
        send_ref[8 - 8 * zh + d] = scr_ref[...].astype(BF)


def coef_kernel(mine_ref, coef_ref, wr_ref, scr_ref, par_ref, log_ref):
    core, y, zh, x = (lax.axis_index(axis) for axis in ("core", "y", "zh", "x"))
    for z in range(8):
        scr_ref[z * 40 : (z + 1) * 40, :] = mine_ref[8 - 8 * zh + z].astype(F32)[56:96]
    sub = lax.broadcasted_iota(jnp.int32, (8, 128), 0)
    grp = lax.broadcasted_iota(jnp.int32, (8, 128), 1) // 16
    for v in range(10):
        for h in range(2):
            at = v * 2 + h
            got = scr_ref[pl.ds(at, 8, stride=40), :] + scr_ref[pl.ds(at + 20, 8, stride=40), :]
            for s in (1, 2, 4):
                up = pltpu.roll(pltpu.roll(got, 8 - s, 0), 16 * s, 1)
                down = pltpu.roll(pltpu.roll(got, s, 0), 128 - 16 * s, 1)
                mine, bit = (sub & s) > 0, (grp & s) > 0
                got = jnp.where(mine == bit, got, jnp.where(mine, down, up))
            par_ref[v, h * 8 : h * 8 + 8, :] = got
    same = mine_ref[zh * 8].astype(F32)
    same = same + pltpu.roll(same, 120, 1)
    other = mine_ref[8 - 8 * zh].astype(F32)
    other = other + pltpu.roll(other, 120, 1)
    for g in range(8):
        log_ref[40 + g * 20 : 60 + g * 20, :] = pltpu.roll(same, (128 - g * 16) % 128, 1)[80:100]
        at = g * 10 if g < 4 else 160 + g * 10
        log_ref[at : at + 10, :] = pltpu.roll(other, (128 - g * 16) % 128, 1)[40:50]
    cols = [log_ref[:, j : j + 1] for j in range(8)]
    for n, (o, i) in enumerate(ARRIVAL):
        dy, dx = jnp.where(core == 0, OFFS[o], OFFS[i]), jnp.where(core == 0, OFFS[i], OFFS[o])
        p = ((y + dy) & 3) * 4 + ((x + dx) & 3)
        for v in range(2):
            wr_ref[v, n : n + 1, :] = par_ref[v, pl.ds(p, 1), :]
        acc = cols[0] * par_ref[2, pl.ds(p, 1), :]
        for j in range(1, 8):
            acc = acc + cols[j] * par_ref[2 + j, pl.ds(p, 1), :]
        coef_ref[n] = jnp.exp(acc)


def state_kernel(mine_ref, theirs_ref, state_ref, scr_ref):
    first = jnp.zeros((1, 128), jnp.int32) + lax.axis_index("core") == 0
    zh = lax.axis_index("zh")
    for z in range(8):
        for at, rows, lo, hi in ((zh * 8 + z, 80, 40, 120), (8 - 8 * zh + z, 40, 0, 200)):
            mine, theirs = mine_ref[at].astype(F32)[0:rows], theirs_ref[at].astype(F32)[0:rows]
            zero, one = jnp.where(first, mine, theirs), jnp.where(first, theirs, mine)
            scr_ref[lo : lo + rows, :] = halves(zero, swapped(one))
            scr_ref[hi : hi + rows, :] = halves(swapped(zero), one)
        state_ref[:, z * 128 : (z + 1) * 128] = scr_ref[...].astype(BF)


def drive(f_ref, h, coef_ref, c, rows, skip, rate, weight):
    def f(d):
        return f_ref[h, 20 + d : 20 + d + rows, :]

    def k(d):
        return coef_ref[c, skip + 20 + d : skip + 20 + d + rows, :]

    mid, kmid = f(0), k(0)
    total = (kmid + k(-20)) * (f(-20) - mid)
    for d in (20, -1, 1):
        total = total + (kmid + k(d)) * (f(d) - mid)
    total = total + rate * (mid - mid * mid * mid)
    return (weight * total).astype(BF)


def sweep(state, basis_refs, coef_ref, wr_ref, f_ref, acc_ref, rows, skip, c=0):
    for ref in basis_refs:
        block = ref[...]
        field = lax.dot_general(state, block, (((1,), (1,)), ((), ())), preferred_element_type=F32)
        parts = []
        for h in range(2):
            f_ref[h, : field.shape[0], :] = field[:, h * 128 : (h + 1) * 128]
            weight, rate = wr_ref[0, c : c + 1, :], wr_ref[1, c : c + 1, :]
            parts.append(drive(f_ref, h, coef_ref, c, rows, skip, rate, weight))
            c += 1
        acc_ref[...] += jnp.dot(jnp.concatenate(parts, axis=1), block, preferred_element_type=F32)


def first_kernel(*refs):
    blocks, (state_ref, coef_ref, wr_ref, out_ref, f_ref, acc_ref) = refs[:8], refs[8:]
    acc_ref[...] = jnp.zeros_like(acc_ref)
    sweep(state_ref[...], blocks, coef_ref, wr_ref, f_ref, acc_ref, 200, 0)
    out_ref[...] = acc_ref[...].astype(BF)


def second_kernel(*refs):
    blocks, (state_ref, coef_ref, wr_ref, own_ref, other_ref, out_ref, f_ref, acc_ref) = refs[:8], refs[8:]
    total = own_ref[...].astype(F32) + other_ref[...].astype(F32)
    now = state_ref[...].astype(F32)[20:220]
    cell = lax.broadcasted_iota(jnp.int32, (200, 128), 0).astype(F32)
    row = jnp.floor((cell + 0.5) * 0.05)
    col = cell - 20.0 * row
    zl, _, y, zh, x = (lax.axis_index(axis) for axis in ALL)
    low = jnp.where((y == 0) & (zh == 0), 1.0, 0.0)
    high = jnp.where((y == 3) & (zh == 1), 8.0, 9.0)
    left = jnp.where((x == 0) & (zl == 0), 2.0, 0.0)
    right = jnp.where((x == 3) & (zl == 7), 17.0, 19.0)
    inside = (row >= low) & (row <= high) & (col >= left) & (col <= right)
    keep = jnp.where(inside, 1.0, 0.0)[:, 0:1]
    state = ((now + STEP * total) * keep).astype(BF)
    acc_ref[...] = jnp.zeros_like(acc_ref)
    sweep(state, blocks, coef_ref, wr_ref, f_ref, acc_ref, 160, 20)
    for z in range(8):
        for y in range(4):
            low = acc_ref[y * 20 + 2 : y * 20 + 18, z * 128 : (z + 1) * 128]
            high = acc_ref[y * 20 + 82 : y * 20 + 98, z * 128 : (z + 1) * 128]
            out_ref[2 * z, y * 16 : y * 16 + 16, :] = halves(low, swapped(high)).astype(BF)
            out_ref[2 * z + 1, y * 16 : y * 16 + 16, :] = halves(swapped(low), high).astype(BF)


def finish_kernel(back_ref, modes_ref, out_ref, scr_ref):
    for y in range(4):
        parts = [
            back_ref[2 * z, y * 16 : y * 16 + 16, :].astype(F32) + back_ref[2 * z + 1, y * 16 : y * 16 + 16, :].astype(F32)
            for z in range(8)
        ]
        turned = jnp.concatenate(parts, axis=0).T
        scr_ref[pl.ds(y, 64, stride=8), :] = turned[0:64]
        scr_ref[pl.ds(y + 4, 64, stride=8), :] = turned[64:128]
    out_ref[...] = modes_ref[...].astype(F32) + STEP * scr_ref[...]


SMEM = pl.BlockSpec(memory_space=pltpu.SMEM)
WHOLE = pl.BlockSpec(memory_space=pltpu.VMEM)


def call(kernel, outs, scratch, scalars, *args):
    specs = [SMEM] * scalars + [WHOLE] * (len(args) - scalars)
    if kernel in (first_kernel, second_kernel):
        args = [pltpu.with_memory_space_constraint(a, pltpu.VMEM) if a.size >= 1 << 17 else a for a in args]
    single = not isinstance(outs, (list, tuple))
    return pl.pallas_call(
        kernel,
        out_shape=outs,
        in_specs=specs,
        out_specs=WHOLE if single else [WHOLE] * len(outs),
        scratch_shapes=scratch,
        compiler_params=pltpu.CompilerParams(vmem_limit_bytes=20 << 20),
    )(*args)


def update(modes_now, basis_rows, quad_weights, germ_nodes, log_fields, reaction_rates):
    y, x = lax.axis_index("y"), lax.axis_index("x")

    part = lax.dynamic_slice_in_dim(basis_rows, (y * 4 + x) * 16, 16, axis=0)
    send = jnp.broadcast_to(part[None], (8, 16, 1024))
    shard = lax.all_to_all(send, "zl", 0, 0, tiled=True).reshape(128, 1024)

    modes, logs = modes_now.reshape(512, 128), log_fields.reshape(64, 128)
    scratch = [VM((512, 128), F32), VM((64, 128), F32)]
    rows = call(rows_kernel, shape((160, 128), BF), scratch, 0, modes, logs)

    def toward(zl, core, y, zh, x):
        return zl, core, y + 2 * zh - 1, zh, x

    got = lax.ppermute(rows, ALL, shift(toward))
    chan = call(channels_kernel, shape((8, 128, 128), F32), scratch, 0, modes, logs)
    full, last, lead = call(
        edges_kernel,
        [shape((10, 144, 128), F32), shape((80, 128), BF), shape((80, 128), BF)],
        [],
        0,
        chan,
        got,
    )
    right = [(i, i + 1) for i in range(3)]
    from_left = lax.ppermute(last, "x", right)
    from_right = lax.ppermute(lead, "x", [(j, i) for i, j in right])
    pars = jnp.concatenate([quad_weights[None], reaction_rates[None], germ_nodes.T], axis=0).reshape(20, 128)
    patch = call(
        patches_kernel,
        shape((16, 104, 128), BF),
        [VM((10, 144, 128), F32), VM((160, 128), F32), VM((104, 128), F32)],
        0,
        full,
        from_left,
        from_right,
        pars,
    )
    mine = lax.all_to_all(patch, ("zh", "zl"), 0, 0, tiled=True)
    theirs = lax.ppermute(mine, "core", [(0, 1), (1, 0)])

    fwd, bwd = plane_shift(0, 1), plane_shift(0, -1)
    less = lax.ppermute(shard, ALL, fwd)
    more = lax.ppermute(shard, ALL, bwd)
    near = jnp.concatenate([shard, less], axis=0)
    far = lax.ppermute(less, ALL, fwd)
    fwd, bwd = plane_shift(1, 1), plane_shift(1, -1)
    near_less = lax.ppermute(near, ALL, fwd)
    near_more = lax.ppermute(near, ALL, bwd)
    away = jnp.concatenate([more, far], axis=0)
    away_more = lax.ppermute(away, ALL, bwd)
    away_less = lax.ppermute(away, ALL, fwd)
    near_far = lax.ppermute(near_less, ALL, fwd)
    away_far = lax.ppermute(away_more, ALL, bwd)
    blocks = (near, away, near_less, near_more, away_less, away_more, near_far, away_far)

    coef, wr = call(
        coef_kernel,
        [shape((16, 240, 128), F32), shape((2, 16, 128), F32)],
        [VM((320, 128), F32), VM((10, 16, 128), F32), VM((240, 128), F32)],
        0,
        mine,
    )
    state = call(state_kernel, shape((240, 1024), BF), [VM((240, 128), F32)], 0, mine, theirs)
    scratch = [VM((2, 240, 128), F32), VM((200, 1024), F32)]
    own = call(first_kernel, shape((200, 1024), BF), scratch, 0, *blocks, state, coef, wr)
    other = lax.ppermute(own, "core", [(0, 1), (1, 0)])
    scratch = [VM((2, 200, 128), F32), VM((160, 1024), F32)]
    out = call(second_kernel, shape((16, 64, 128), BF), scratch, 0, *blocks, state, coef, wr, own, other)
    back = lax.all_to_all(out, ("zl", "core"), 0, 0, tiled=True)
    result = call(finish_kernel, shape((512, 128), F32), [VM((512, 128), F32)], 0, back, modes)
    return result.reshape(64, 8, 128)


def solution(mesh):
    fine = Mesh(mesh.devices.reshape(SPLIT), ALL)
    quad = ("zl", "core")
    in_specs = (P(quad, ("y", "zh"), "x"), P(quad, None), P(quad), P(quad, None), P(None, ("y", "zh"), "x"), P(quad))
    out_specs = P(quad, ("y", "zh"), "x")
    return jax.shard_map(update, mesh=fine, in_specs=in_specs, out_specs=out_specs, check_vma=False)
```

```python
import itertools

import jax
import jax.numpy as jnp
from jax import lax
from jax.experimental import pallas as pl
from jax.experimental.pallas import tpu as pltpu
from jax.sharding import Mesh
from jax.sharding import PartitionSpec as P


STEP = 0.04
BF = jnp.bfloat16
F32 = jnp.float32
VM = pltpu.VMEM
OFFS = (0, -1, 1, 2)
ARRIVAL = tuple((o, i) for o, half in ((0, 0), (0, 2), (1, 0), (2, 0), (1, 2), (2, 2), (3, 0), (3, 2)) for i in (half, half + 1))
ALL = ("zl", "core", "y", "zh", "x")
SPLIT = (8, 2, 4, 2, 4)


def shift(moves):
    every = list(itertools.product(*map(range, SPLIT)))
    number = {at: i for i, at in enumerate(every)}
    pairs = ((number[at], number.get(moves(*at))) for at in every)
    return [(i, j) for i, j in pairs if j is not None]


def plane_shift(phase, step):
    def moves(zl, core, y, zh, x):
        if (core + phase) % 2 == 0:
            return zl, core, y, zh, (x + step) % 4
        return zl, core, (y + step) % 4, zh, x

    return shift(moves)


def shape(dims, kind):
    return jax.ShapeDtypeStruct(dims, kind)


def halves(low, high):
    lane = lax.broadcasted_iota(jnp.int32, low.shape, 1)
    return jnp.where(lane < 64, low, high)


def swapped(x):
    return pltpu.roll(x, 64, 1)


def rows_kernel(modes_ref, logs_ref, out_ref, scr_ref, log_ref):
    scr_ref[...] = modes_ref[...].astype(F32)
    log_ref[...] = logs_ref[...]
    upper = jnp.zeros((1, 128), jnp.int32) + lax.axis_index("zh") == 0
    for k in range(2):
        logs = jnp.where(upper, log_ref[pl.ds(k, 8, stride=8), :], log_ref[pl.ds(6 + k, 8, stride=8), :])
        high = logs.astype(BF).astype(F32)
        block = jnp.where(upper, scr_ref[pl.ds(k, 64, stride=8), :], scr_ref[pl.ds(6 + k, 64, stride=8), :])
        out_ref[k * 80 : k * 80 + 80, :] = jnp.concatenate([block, high, logs - high], axis=0).astype(BF)


def channels_kernel(modes_ref, logs_ref, chan_ref, scr_ref, log_ref):
    scr_ref[...] = modes_ref[...].astype(F32)
    log_ref[...] = logs_ref[...]
    zeros = jnp.zeros((48, 128), F32)
    for y in range(8):
        block = scr_ref[pl.ds(y, 64, stride=8), :]
        logs = log_ref[pl.ds(y, 8, stride=8), :]
        high = logs.astype(BF).astype(F32)
        chan_ref[y] = jnp.concatenate([block, high, logs - high, zeros], axis=0).T


def edges_kernel(chan_ref, got_ref, full_ref, last_ref, lead_ref):
    lower = lax.axis_index("zh")
    zeros = jnp.zeros((48, 128), F32)
    got = got_ref[...].astype(F32)
    for k in range(2):
        full_ref[8 - 8 * lower + k, 8:136, :] = jnp.concatenate([got[k * 80 : k * 80 + 80], zeros], axis=0).T
    for r in range(8):
        full_ref[2 * lower + r, 8:136, :] = chan_ref[r]
    for r in range(10):
        last_ref[r * 8 : r * 8 + 8] = full_ref[r, 128:136, :].astype(BF)
        lead_ref[r * 8 : r * 8 + 8] = full_ref[r, 8:16, :].astype(BF)


def log_rows(cell_ref, rows):
    lane = lax.broadcasted_iota(jnp.int32, (rows, 128), 1)
    logs = jnp.zeros((rows, 128), F32)
    for g in range(8):
        piece = pltpu.roll(cell_ref[g * rows : (g + 1) * rows, :], (g * 16 - 64) % 128, 1)
        logs = jnp.where((lane >= g * 16) & (lane < g * 16 + 16), piece, logs)
    return logs


def patches_kernel(full_ref, left_ref, right_ref, pars_ref, send_ref, wide_ref, cell_ref, scr_ref):
    left, right = left_ref[...].astype(F32), right_ref[...].astype(F32)
    for r in range(10):
        wide_ref[r, 0:8, :] = left[r * 8 : r * 8 + 8]
        wide_ref[r, 8:136, :] = full_ref[r, 8:136, :]
        wide_ref[r, 136:144, :] = right[r * 8 : r * 8 + 8]
    zh = lax.axis_index("zh")
    scr_ref[...] = jnp.zeros_like(scr_ref)
    for d in range(8):
        for r in range(8):
            cell_ref[r * 20 : r * 20 + 20, :] = wide_ref[2 * zh + r, 16 * d + 6 : 16 * d + 26, :]
        scr_ref[0:80, :] = halves(cell_ref[0:80, :], swapped(cell_ref[80:160, :]))
        scr_ref[80:100, :] = log_rows(cell_ref, 20)
        send_ref[zh * 8 + d] = scr_ref[...].astype(BF)
    pars = pars_ref[...]
    high = pars.astype(BF).astype(F32)
    scr_ref[56:76, :] = high
    scr_ref[76:96, :] = pars - high
    for d in range(8):
        for r in range(4):
            cell_ref[r * 20 : r * 20 + 20, :] = wide_ref[6 - 6 * zh + r, 16 * d + 6 : 16 * d + 26, :]
        scr_ref[0:40, :] = halves(cell_ref[0:40, :], swapped(cell_ref[40:80, :]))
        scr_ref[40:50, :] = log_rows(cell_ref, 10)
        send_ref[8 - 8 * zh + d] = scr_ref[...].astype(BF)


def coef_kernel(mine_ref, coef_ref, wr_ref, scr_ref, par_ref, log_ref):
    core, y, zh, x = (lax.axis_index(axis) for axis in ("core", "y", "zh", "x"))
    for z in range(8):
        scr_ref[z * 40 : (z + 1) * 40, :] = mine_ref[8 - 8 * zh + z].astype(F32)[56:96]
    sub = lax.broadcasted_iota(jnp.int32, (8, 128), 0)
    grp = lax.broadcasted_iota(jnp.int32, (8, 128), 1) // 16
    for v in range(10):
        for h in range(2):
            at = v * 2 + h
            got = scr_ref[pl.ds(at, 8, stride=40), :] + scr_ref[pl.ds(at + 20, 8, stride=40), :]
            for s in (1, 2, 4):
                up = pltpu.roll(pltpu.roll(got, 8 - s, 0), 16 * s, 1)
                down = pltpu.roll(pltpu.roll(got, s, 0), 128 - 16 * s, 1)
                mine, bit = (sub & s) > 0, (grp & s) > 0
                got = jnp.where(mine == bit, got, jnp.where(mine, down, up))
            par_ref[v, h * 8 : h * 8 + 8, :] = got
    same = mine_ref[zh * 8].astype(F32)
    same = same + pltpu.roll(same, 120, 1)
    other = mine_ref[8 - 8 * zh].astype(F32)
    other = other + pltpu.roll(other, 120, 1)
    for g in range(8):
        log_ref[40 + g * 20 : 60 + g * 20, :] = pltpu.roll(same, (128 - g * 16) % 128, 1)[80:100]
        at = g * 10 if g < 4 else 160 + g * 10
        log_ref[at : at + 10, :] = pltpu.roll(other, (128 - g * 16) % 128, 1)[40:50]
    cols = [log_ref[:, j : j + 1] for j in range(8)]
    for n, (o, i) in enumerate(ARRIVAL):
        dy, dx = jnp.where(core == 0, OFFS[o], OFFS[i]), jnp.where(core == 0, OFFS[i], OFFS[o])
        p = ((y + dy) & 3) * 4 + ((x + dx) & 3)
        for v in range(2):
            wr_ref[v, n : n + 1, :] = par_ref[v, pl.ds(p, 1), :]
        acc = cols[0] * par_ref[2, pl.ds(p, 1), :]
        for j in range(1, 8):
            acc = acc + cols[j] * par_ref[2 + j, pl.ds(p, 1), :]
        coef_ref[n] = jnp.exp(acc)


def state_kernel(mine_ref, theirs_ref, state_ref, scr_ref):
    first = jnp.zeros((1, 128), jnp.int32) + lax.axis_index("core") == 0
    zh = lax.axis_index("zh")
    for z in range(8):
        for at, rows, lo, hi in ((zh * 8 + z, 80, 40, 120), (8 - 8 * zh + z, 40, 0, 200)):
            mine, theirs = mine_ref[at].astype(F32)[0:rows], theirs_ref[at].astype(F32)[0:rows]
            zero, one = jnp.where(first, mine, theirs), jnp.where(first, theirs, mine)
            scr_ref[lo : lo + rows, :] = halves(zero, swapped(one))
            scr_ref[hi : hi + rows, :] = halves(swapped(zero), one)
        state_ref[:, z * 128 : (z + 1) * 128] = scr_ref[...].astype(BF)


def drive(f_ref, h, coef_ref, c, rows, skip, rate, weight):
    def f(d):
        return f_ref[h, 20 + d : 20 + d + rows, :]

    def k(d):
        return coef_ref[c, skip + 20 + d : skip + 20 + d + rows, :]

    mid, kmid = f(0), k(0)
    total = (kmid + k(-20)) * (f(-20) - mid)
    for d in (20, -1, 1):
        total = total + (kmid + k(d)) * (f(d) - mid)
    total = total + rate * (mid - mid * mid * mid)
    return (weight * total).astype(BF)


def sweep(state, basis_refs, coef_ref, wr_ref, f_ref, acc_ref, rows, skip, c=0):
    for ref in basis_refs:
        block = ref[...]
        field = lax.dot_general(state, block, (((1,), (1,)), ((), ())), preferred_element_type=F32)
        parts = []
        for h in range(2):
            f_ref[h, : field.shape[0], :] = field[:, h * 128 : (h + 1) * 128]
            weight, rate = wr_ref[0, c : c + 1, :], wr_ref[1, c : c + 1, :]
            parts.append(drive(f_ref, h, coef_ref, c, rows, skip, rate, weight))
            c += 1
        acc_ref[...] += jnp.dot(jnp.concatenate(parts, axis=1), block, preferred_element_type=F32)


def first_kernel(*refs):
    blocks, (state_ref, coef_ref, wr_ref, out_ref, f_ref, acc_ref) = refs[:8], refs[8:]
    acc_ref[...] = jnp.zeros_like(acc_ref)
    sweep(state_ref[...], blocks, coef_ref, wr_ref, f_ref, acc_ref, 200, 0)
    out_ref[...] = acc_ref[...].astype(BF)


def second_kernel(*refs):
    blocks, (state_ref, coef_ref, wr_ref, own_ref, other_ref, kept_ref, sent_ref, f_ref, acc_ref) = refs[:8], refs[8:]
    total = own_ref[...].astype(F32) + other_ref[...].astype(F32)
    now = state_ref[...].astype(F32)[20:220]
    cell = lax.broadcasted_iota(jnp.int32, (200, 128), 0).astype(F32)
    row = jnp.floor((cell + 0.5) * 0.05)
    col = cell - 20.0 * row
    zl, _, y, zh, x = (lax.axis_index(axis) for axis in ALL)
    low = jnp.where((y == 0) & (zh == 0), 1.0, 0.0)
    high = jnp.where((y == 3) & (zh == 1), 8.0, 9.0)
    left = jnp.where((x == 0) & (zl == 0), 2.0, 0.0)
    right = jnp.where((x == 3) & (zl == 7), 17.0, 19.0)
    inside = (row >= low) & (row <= high) & (col >= left) & (col <= right)
    keep = jnp.where(inside, 1.0, 0.0)[:, 0:1]
    state = ((now + STEP * total) * keep).astype(BF)
    acc_ref[...] = jnp.zeros_like(acc_ref)
    sweep(state, blocks, coef_ref, wr_ref, f_ref, acc_ref, 160, 20)
    first = jnp.zeros((1, 128), jnp.int32) + lax.axis_index("core") == 0
    for z in range(8):
        for y in range(4):
            low = acc_ref[y * 20 + 2 : y * 20 + 18, z * 128 : (z + 1) * 128]
            high = acc_ref[y * 20 + 82 : y * 20 + 98, z * 128 : (z + 1) * 128]
            zero, one = halves(low, swapped(high)), halves(swapped(low), high)
            kept_ref[z, y * 16 : y * 16 + 16, :] = jnp.where(first, zero, one)
            sent_ref[z, y * 16 : y * 16 + 16, :] = jnp.where(first, one, zero).astype(BF)


def add_kernel(kept_ref, got_ref, out_ref):
    out_ref[...] = (kept_ref[...] + got_ref[...].astype(F32)).astype(BF)


def finish_kernel(back_ref, modes_ref, out_ref, scr_ref):
    for y in range(4):
        parts = [
            back_ref[z, y * 16 : y * 16 + 16, :].astype(F32) for z in range(8)
        ]
        turned = jnp.concatenate(parts, axis=0).T
        scr_ref[pl.ds(y, 64, stride=8), :] = turned[0:64]
        scr_ref[pl.ds(y + 4, 64, stride=8), :] = turned[64:128]
    out_ref[...] = modes_ref[...].astype(F32) + STEP * scr_ref[...]


SMEM = pl.BlockSpec(memory_space=pltpu.SMEM)
WHOLE = pl.BlockSpec(memory_space=pltpu.VMEM)


def call(kernel, outs, scratch, scalars, *args):
    specs = [SMEM] * scalars + [WHOLE] * (len(args) - scalars)
    if kernel in (first_kernel, second_kernel):
        args = [pltpu.with_memory_space_constraint(a, pltpu.VMEM) if a.size >= 1 << 17 else a for a in args]
    single = not isinstance(outs, (list, tuple))
    return pl.pallas_call(
        kernel,
        out_shape=outs,
        in_specs=specs,
        out_specs=WHOLE if single else [WHOLE] * len(outs),
        scratch_shapes=scratch,
        compiler_params=pltpu.CompilerParams(vmem_limit_bytes=20 << 20),
    )(*args)


def update(modes_now, basis_rows, quad_weights, germ_nodes, log_fields, reaction_rates):
    y, x = lax.axis_index("y"), lax.axis_index("x")

    part = lax.dynamic_slice_in_dim(basis_rows, (y * 4 + x) * 16, 16, axis=0)
    send = jnp.broadcast_to(part[None], (8, 16, 1024))
    shard = lax.all_to_all(send, "zl", 0, 0, tiled=True).reshape(128, 1024)

    modes, logs = modes_now.reshape(512, 128), log_fields.reshape(64, 128)
    scratch = [VM((512, 128), F32), VM((64, 128), F32)]
    rows = call(rows_kernel, shape((160, 128), BF), scratch, 0, modes, logs)

    def toward(zl, core, y, zh, x):
        return zl, core, y + 2 * zh - 1, zh, x

    got = lax.ppermute(rows, ALL, shift(toward))
    chan = call(channels_kernel, shape((8, 128, 128), F32), scratch, 0, modes, logs)
    full, last, lead = call(
        edges_kernel,
        [shape((10, 144, 128), F32), shape((80, 128), BF), shape((80, 128), BF)],
        [],
        0,
        chan,
        got,
    )
    right = [(i, i + 1) for i in range(3)]
    from_left = lax.ppermute(last, "x", right)
    from_right = lax.ppermute(lead, "x", [(j, i) for i, j in right])
    pars = jnp.concatenate([quad_weights[None], reaction_rates[None], germ_nodes.T], axis=0).reshape(20, 128)
    patch = call(
        patches_kernel,
        shape((16, 104, 128), BF),
        [VM((10, 144, 128), F32), VM((160, 128), F32), VM((104, 128), F32)],
        0,
        full,
        from_left,
        from_right,
        pars,
    )
    mine = lax.all_to_all(patch, ("zh", "zl"), 0, 0, tiled=True)
    theirs = lax.ppermute(mine, "core", [(0, 1), (1, 0)])

    fwd, bwd = plane_shift(0, 1), plane_shift(0, -1)
    less = lax.ppermute(shard, ALL, fwd)
    more = lax.ppermute(shard, ALL, bwd)
    near = jnp.concatenate([shard, less], axis=0)
    far = lax.ppermute(shard, ALL, plane_shift(0, 2))
    fwd, bwd = plane_shift(1, 1), plane_shift(1, -1)
    near_less = lax.ppermute(near, ALL, fwd)
    near_more = lax.ppermute(near, ALL, bwd)
    away = jnp.concatenate([more, far], axis=0)
    away_more = lax.ppermute(away, ALL, bwd)
    away_less = lax.ppermute(away, ALL, fwd)
    near_far = lax.ppermute(near_less, ALL, fwd)
    away_far = lax.ppermute(away_more, ALL, bwd)
    blocks = (near, away, near_less, near_more, away_less, away_more, near_far, away_far)

    coef, wr = call(
        coef_kernel,
        [shape((16, 240, 128), F32), shape((2, 16, 128), F32)],
        [VM((320, 128), F32), VM((10, 16, 128), F32), VM((240, 128), F32)],
        0,
        mine,
    )
    state = call(state_kernel, shape((240, 1024), BF), [VM((240, 128), F32)], 0, mine, theirs)
    scratch = [VM((2, 240, 128), F32), VM((200, 1024), F32)]
    own = call(first_kernel, shape((200, 1024), BF), scratch, 0, *blocks, state, coef, wr)
    other = lax.ppermute(own, "core", [(0, 1), (1, 0)])
    scratch = [VM((2, 200, 128), F32), VM((160, 1024), F32)]
    outs = [shape((8, 64, 128), F32), shape((8, 64, 128), BF)]
    kept, sent = call(second_kernel, outs, scratch, 0, *blocks, state, coef, wr, own, other)
    got = lax.ppermute(sent, "core", [(0, 1), (1, 0)])
    out = call(add_kernel, shape((8, 64, 128), BF), [], 0, kept, got)
    back = lax.all_to_all(out, "zl", 0, 0, tiled=True)
    result = call(finish_kernel, shape((512, 128), F32), [VM((512, 128), F32)], 0, back, modes)
    return result.reshape(64, 8, 128)


def solution(mesh):
    fine = Mesh(mesh.devices.reshape(SPLIT), ALL)
    quad = ("zl", "core")
    in_specs = (P(quad, ("y", "zh"), "x"), P(quad, None), P(quad), P(quad, None), P(None, ("y", "zh"), "x"), P(quad))
    out_specs = P(quad, ("y", "zh"), "x")
    return jax.shard_map(update, mesh=fine, in_specs=in_specs, out_specs=out_specs, check_vma=False)
```

```python
import itertools

import jax
import jax.numpy as jnp
from jax import lax
from jax.experimental import pallas as pl
from jax.experimental.pallas import tpu as pltpu
from jax.sharding import Mesh
from jax.sharding import PartitionSpec as P


STEP = 0.04
BF = jnp.bfloat16
F32 = jnp.float32
VM = pltpu.VMEM
OFFS = (0, -1, 1, 2)
ARRIVAL = tuple((o, i) for o, half in ((0, 0), (0, 2), (1, 0), (2, 0), (1, 2), (2, 2), (3, 0), (3, 2)) for i in (half, half + 1))
CHIPS = (0, 4, 2, 6, 1, 5, 3, 7)
ALL = ("zl", "core", "y", "zh", "x")
SPLIT = (8, 2, 4, 2, 4)


def shift(moves):
    every = list(itertools.product(*map(range, SPLIT)))
    number = {at: i for i, at in enumerate(every)}
    pairs = ((number[at], number.get(moves(*at))) for at in every)
    return [(i, j) for i, j in pairs if j is not None]


def plane_shift(phase, step):
    def moves(zl, core, y, zh, x):
        if (core + phase) % 2 == 0:
            return zl, core, y, zh, (x + step) % 4
        return zl, core, (y + step) % 4, zh, x

    return shift(moves)


def shape(dims, kind):
    return jax.ShapeDtypeStruct(dims, kind)


def halves(low, high):
    lane = lax.broadcasted_iota(jnp.int32, low.shape, 1)
    return jnp.where(lane < 64, low, high)


def swapped(x):
    return pltpu.roll(x, 64, 1)


def rows_kernel(modes_ref, logs_ref, out_ref, scr_ref, log_ref):
    scr_ref[...] = modes_ref[...].astype(F32)
    log_ref[...] = logs_ref[...]
    upper = jnp.zeros((1, 128), jnp.int32) + lax.axis_index("zh") == 0
    for k in range(2):
        logs = jnp.where(upper, log_ref[pl.ds(k, 8, stride=8), :], log_ref[pl.ds(6 + k, 8, stride=8), :])
        high = logs.astype(BF).astype(F32)
        block = jnp.where(upper, scr_ref[pl.ds(k, 64, stride=8), :], scr_ref[pl.ds(6 + k, 64, stride=8), :])
        out_ref[k * 80 : k * 80 + 80, :] = jnp.concatenate([block, high, logs - high], axis=0).astype(BF)


def channels_kernel(modes_ref, logs_ref, chan_ref, scr_ref, log_ref):
    scr_ref[...] = modes_ref[...].astype(F32)
    log_ref[...] = logs_ref[...]
    zeros = jnp.zeros((48, 128), F32)
    for y in range(8):
        block = scr_ref[pl.ds(y, 64, stride=8), :]
        logs = log_ref[pl.ds(y, 8, stride=8), :]
        high = logs.astype(BF).astype(F32)
        chan_ref[y] = jnp.concatenate([block, high, logs - high, zeros], axis=0).T


def edges_kernel(chan_ref, got_ref, full_ref, last_ref, lead_ref):
    lower = lax.axis_index("zh")
    zeros = jnp.zeros((48, 128), F32)
    got = got_ref[...].astype(F32)
    for k in range(2):
        full_ref[8 - 8 * lower + k, 8:136, :] = jnp.concatenate([got[k * 80 : k * 80 + 80], zeros], axis=0).T
    for r in range(8):
        full_ref[2 * lower + r, 8:136, :] = chan_ref[r]
    for r in range(10):
        last_ref[r * 8 : r * 8 + 8] = full_ref[r, 128:136, :].astype(BF)
        lead_ref[r * 8 : r * 8 + 8] = full_ref[r, 8:16, :].astype(BF)


def log_rows(cell_ref, rows):
    lane = lax.broadcasted_iota(jnp.int32, (rows, 128), 1)
    logs = jnp.zeros((rows, 128), F32)
    for g in range(8):
        piece = pltpu.roll(cell_ref[g * rows : (g + 1) * rows, :], (g * 16 - 64) % 128, 1)
        logs = jnp.where((lane >= g * 16) & (lane < g * 16 + 16), piece, logs)
    return logs


def patches_kernel(full_ref, left_ref, right_ref, pars_ref, send_ref, wide_ref, cell_ref, scr_ref):
    left, right = left_ref[...].astype(F32), right_ref[...].astype(F32)
    for r in range(10):
        wide_ref[r, 0:8, :] = left[r * 8 : r * 8 + 8]
        wide_ref[r, 8:136, :] = full_ref[r, 8:136, :]
        wide_ref[r, 136:144, :] = right[r * 8 : r * 8 + 8]
    zh = lax.axis_index("zh")
    scr_ref[...] = jnp.zeros_like(scr_ref)
    for d in range(8):
        for r in range(8):
            cell_ref[r * 20 : r * 20 + 20, :] = wide_ref[2 * zh + r, 16 * d + 6 : 16 * d + 26, :]
        scr_ref[0:80, :] = halves(cell_ref[0:80, :], swapped(cell_ref[80:160, :]))
        scr_ref[80:100, :] = log_rows(cell_ref, 20)
        send_ref[zh * 8 + d] = scr_ref[...].astype(BF)
    pars = pars_ref[...]
    high = pars.astype(BF).astype(F32)
    scr_ref[56:76, :] = high
    scr_ref[76:96, :] = pars - high
    for d in range(8):
        for r in range(4):
            cell_ref[r * 20 : r * 20 + 20, :] = wide_ref[6 - 6 * zh + r, 16 * d + 6 : 16 * d + 26, :]
        scr_ref[0:40, :] = halves(cell_ref[0:40, :], swapped(cell_ref[40:80, :]))
        scr_ref[40:50, :] = log_rows(cell_ref, 10)
        send_ref[8 - 8 * zh + d] = scr_ref[...].astype(BF)


def coef_kernel(mine_ref, coef_ref, wr_ref, scr_ref, par_ref, log_ref):
    core, y, zh, x = (lax.axis_index(axis) for axis in ("core", "y", "zh", "x"))
    zl = lax.axis_index("zl")
    for z in range(8):
        scr_ref[z * 40 : (z + 1) * 40, :] = mine_ref[8 - 8 * zh + (zl ^ CHIPS[z])].astype(F32)[56:96]
    sub = lax.broadcasted_iota(jnp.int32, (8, 128), 0)
    grp = lax.broadcasted_iota(jnp.int32, (8, 128), 1) // 16
    for v in range(10):
        for h in range(2):
            at = v * 2 + h
            got = scr_ref[pl.ds(at, 8, stride=40), :] + scr_ref[pl.ds(at + 20, 8, stride=40), :]
            for s in (1, 2, 4):
                up = pltpu.roll(pltpu.roll(got, 8 - s, 0), 16 * s, 1)
                down = pltpu.roll(pltpu.roll(got, s, 0), 128 - 16 * s, 1)
                mine, bit = (sub & s) > 0, (grp & s) > 0
                got = jnp.where(mine == bit, got, jnp.where(mine, down, up))
            par_ref[v, h * 8 : h * 8 + 8, :] = got
    same = mine_ref[zh * 8].astype(F32)
    same = same + pltpu.roll(same, 120, 1)
    other = mine_ref[8 - 8 * zh].astype(F32)
    other = other + pltpu.roll(other, 120, 1)
    for g in range(8):
        log_ref[40 + g * 20 : 60 + g * 20, :] = pltpu.roll(same, (128 - g * 16) % 128, 1)[80:100]
        at = g * 10 if g < 4 else 160 + g * 10
        log_ref[at : at + 10, :] = pltpu.roll(other, (128 - g * 16) % 128, 1)[40:50]
    cols = [log_ref[:, j : j + 1] for j in range(8)]
    for n, (o, i) in enumerate(ARRIVAL):
        dy, dx = jnp.where(core == 0, OFFS[o], OFFS[i]), jnp.where(core == 0, OFFS[i], OFFS[o])
        p = ((y + dy) & 3) * 4 + ((x + dx) & 3)
        for v in range(2):
            wr_ref[v, n : n + 1, :] = par_ref[v, pl.ds(p, 1), :]
        acc = cols[0] * par_ref[2, pl.ds(p, 1), :]
        for j in range(1, 8):
            acc = acc + cols[j] * par_ref[2 + j, pl.ds(p, 1), :]
        coef_ref[n] = jnp.exp(acc)


def state_kernel(mine_ref, theirs_ref, state_ref, scr_ref):
    first = jnp.zeros((1, 128), jnp.int32) + lax.axis_index("core") == 0
    zh = lax.axis_index("zh")
    for z in range(8):
        for at, rows, lo, hi in ((zh * 8 + z, 80, 40, 120), (8 - 8 * zh + z, 40, 0, 200)):
            mine, theirs = mine_ref[at].astype(F32)[0:rows], theirs_ref[at].astype(F32)[0:rows]
            zero, one = jnp.where(first, mine, theirs), jnp.where(first, theirs, mine)
            scr_ref[lo : lo + rows, :] = halves(zero, swapped(one))
            scr_ref[hi : hi + rows, :] = halves(swapped(zero), one)
        state_ref[:, z * 128 : (z + 1) * 128] = scr_ref[...].astype(BF)


def drive(f_ref, h, coef_ref, c, rows, skip, rate, weight):
    def f(d):
        return f_ref[h, 20 + d : 20 + d + rows, :]

    def k(d):
        return coef_ref[c, skip + 20 + d : skip + 20 + d + rows, :]

    mid, kmid = f(0), k(0)
    total = (kmid + k(-20)) * (f(-20) - mid)
    for d in (20, -1, 1):
        total = total + (kmid + k(d)) * (f(d) - mid)
    total = total + rate * (mid - mid * mid * mid)
    return (weight * total).astype(BF)


def sweep(state, basis_refs, coef_ref, wr_ref, f_ref, acc_ref, rows, skip, c=0):
    for ref in basis_refs:
        block = ref[...]
        field = lax.dot_general(state, block, (((1,), (1,)), ((), ())), preferred_element_type=F32)
        parts = []
        for h in range(2):
            f_ref[h, : field.shape[0], :] = field[:, h * 128 : (h + 1) * 128]
            weight, rate = wr_ref[0, c : c + 1, :], wr_ref[1, c : c + 1, :]
            parts.append(drive(f_ref, h, coef_ref, c, rows, skip, rate, weight))
            c += 1
        acc_ref[...] += jnp.dot(jnp.concatenate(parts, axis=1), block, preferred_element_type=F32)


def first_kernel(*refs):
    blocks, (state_ref, coef_ref, wr_ref, out_ref, f_ref, acc_ref) = refs[:8], refs[8:]
    acc_ref[...] = jnp.zeros_like(acc_ref)
    sweep(state_ref[...], blocks, coef_ref, wr_ref, f_ref, acc_ref, 200, 0)
    out_ref[...] = acc_ref[...].astype(BF)


def second_kernel(*refs):
    blocks, (state_ref, coef_ref, wr_ref, own_ref, other_ref, kept_ref, sent_ref, f_ref, acc_ref) = refs[:8], refs[8:]
    total = own_ref[...].astype(F32) + other_ref[...].astype(F32)
    now = state_ref[...].astype(F32)[20:220]
    cell = lax.broadcasted_iota(jnp.int32, (200, 128), 0).astype(F32)
    row = jnp.floor((cell + 0.5) * 0.05)
    col = cell - 20.0 * row
    zl, _, y, zh, x = (lax.axis_index(axis) for axis in ALL)
    low = jnp.where((y == 0) & (zh == 0), 1.0, 0.0)
    high = jnp.where((y == 3) & (zh == 1), 8.0, 9.0)
    left = jnp.where((x == 0) & (zl == 0), 2.0, 0.0)
    right = jnp.where((x == 3) & (zl == 7), 17.0, 19.0)
    inside = (row >= low) & (row <= high) & (col >= left) & (col <= right)
    keep = jnp.where(inside, 1.0, 0.0)[:, 0:1]
    state = ((now + STEP * total) * keep).astype(BF)
    acc_ref[...] = jnp.zeros_like(acc_ref)
    sweep(state, blocks, coef_ref, wr_ref, f_ref, acc_ref, 160, 20)
    first = jnp.zeros((1, 128), jnp.int32) + lax.axis_index("core") == 0
    for z in range(8):
        for y in range(4):
            low = acc_ref[y * 20 + 2 : y * 20 + 18, z * 128 : (z + 1) * 128]
            high = acc_ref[y * 20 + 82 : y * 20 + 98, z * 128 : (z + 1) * 128]
            zero, one = halves(low, swapped(high)), halves(swapped(low), high)
            kept_ref[z, y * 16 : y * 16 + 16, :] = jnp.where(first, zero, one)
            sent_ref[z, y * 16 : y * 16 + 16, :] = jnp.where(first, one, zero).astype(BF)


def add_kernel(kept_ref, got_ref, out_ref):
    out_ref[...] = (kept_ref[...] + got_ref[...].astype(F32)).astype(BF)


def finish_kernel(back_ref, modes_ref, out_ref, scr_ref):
    for y in range(4):
        parts = [
            back_ref[z, y * 16 : y * 16 + 16, :].astype(F32) for z in range(8)
        ]
        turned = jnp.concatenate(parts, axis=0).T
        scr_ref[pl.ds(y, 64, stride=8), :] = turned[0:64]
        scr_ref[pl.ds(y + 4, 64, stride=8), :] = turned[64:128]
    out_ref[...] = modes_ref[...].astype(F32) + STEP * scr_ref[...]


SMEM = pl.BlockSpec(memory_space=pltpu.SMEM)
WHOLE = pl.BlockSpec(memory_space=pltpu.VMEM)


def call(kernel, outs, scratch, scalars, *args):
    specs = [SMEM] * scalars + [WHOLE] * (len(args) - scalars)
    if kernel in (first_kernel, second_kernel):
        args = [pltpu.with_memory_space_constraint(a, pltpu.VMEM) if a.size >= 1 << 17 else a for a in args]
    single = not isinstance(outs, (list, tuple))
    return pl.pallas_call(
        kernel,
        out_shape=outs,
        in_specs=specs,
        out_specs=WHOLE if single else [WHOLE] * len(outs),
        scratch_shapes=scratch,
        compiler_params=pltpu.CompilerParams(vmem_limit_bytes=20 << 20),
    )(*args)


def update(modes_now, basis_rows, quad_weights, germ_nodes, log_fields, reaction_rates):
    y, x = lax.axis_index("y"), lax.axis_index("x")

    part = lax.dynamic_slice_in_dim(basis_rows, (y * 4 + x) * 16, 16, axis=0)
    shard = part
    for hop in (4, 2, 1):
        got = lax.ppermute(shard, "zl", [(i, i ^ hop) for i in range(8)])
        shard = jnp.concatenate([shard, got], axis=0)

    modes, logs = modes_now.reshape(512, 128), log_fields.reshape(64, 128)
    scratch = [VM((512, 128), F32), VM((64, 128), F32)]
    rows = call(rows_kernel, shape((160, 128), BF), scratch, 0, modes, logs)

    def toward(zl, core, y, zh, x):
        return zl, core, y + 2 * zh - 1, zh, x

    got = lax.ppermute(rows, ALL, shift(toward))
    chan = call(channels_kernel, shape((8, 128, 128), F32), scratch, 0, modes, logs)
    full, last, lead = call(
        edges_kernel,
        [shape((10, 144, 128), F32), shape((80, 128), BF), shape((80, 128), BF)],
        [],
        0,
        chan,
        got,
    )
    right = [(i, i + 1) for i in range(3)]
    from_left = lax.ppermute(last, "x", right)
    from_right = lax.ppermute(lead, "x", [(j, i) for i, j in right])
    pars = jnp.concatenate([quad_weights[None], reaction_rates[None], germ_nodes.T], axis=0).reshape(20, 128)
    patch = call(
        patches_kernel,
        shape((16, 104, 128), BF),
        [VM((10, 144, 128), F32), VM((160, 128), F32), VM((104, 128), F32)],
        0,
        full,
        from_left,
        from_right,
        pars,
    )
    mine = lax.all_to_all(patch, ("zh", "zl"), 0, 0, tiled=True)
    theirs = lax.ppermute(mine, "core", [(0, 1), (1, 0)])

    fwd, bwd = plane_shift(0, 1), plane_shift(0, -1)
    less = lax.ppermute(shard, ALL, fwd)
    more = lax.ppermute(shard, ALL, bwd)
    near = jnp.concatenate([shard, less], axis=0)
    far = lax.ppermute(shard, ALL, plane_shift(0, 2))
    fwd, bwd = plane_shift(1, 1), plane_shift(1, -1)
    near_less = lax.ppermute(near, ALL, fwd)
    near_more = lax.ppermute(near, ALL, bwd)
    away = jnp.concatenate([more, far], axis=0)
    away_more = lax.ppermute(away, ALL, bwd)
    away_less = lax.ppermute(away, ALL, fwd)
    near_far = lax.ppermute(near_less, ALL, fwd)
    away_far = lax.ppermute(away_more, ALL, bwd)
    blocks = (near, away, near_less, near_more, away_less, away_more, near_far, away_far)

    coef, wr = call(
        coef_kernel,
        [shape((16, 240, 128), F32), shape((2, 16, 128), F32)],
        [VM((320, 128), F32), VM((10, 16, 128), F32), VM((240, 128), F32)],
        0,
        mine,
    )
    state = call(state_kernel, shape((240, 1024), BF), [VM((240, 128), F32)], 0, mine, theirs)
    scratch = [VM((2, 240, 128), F32), VM((200, 1024), F32)]
    own = call(first_kernel, shape((200, 1024), BF), scratch, 0, *blocks, state, coef, wr)
    other = lax.ppermute(own, "core", [(0, 1), (1, 0)])
    scratch = [VM((2, 200, 128), F32), VM((160, 1024), F32)]
    outs = [shape((8, 64, 128), F32), shape((8, 64, 128), BF)]
    kept, sent = call(second_kernel, outs, scratch, 0, *blocks, state, coef, wr, own, other)
    got = lax.ppermute(sent, "core", [(0, 1), (1, 0)])
    out = call(add_kernel, shape((8, 64, 128), BF), [], 0, kept, got)
    back = lax.all_to_all(out, "zl", 0, 0, tiled=True)
    result = call(finish_kernel, shape((512, 128), F32), [VM((512, 128), F32)], 0, back, modes)
    return result.reshape(64, 8, 128)


def solution(mesh):
    fine = Mesh(mesh.devices.reshape(SPLIT), ALL)
    quad = ("zl", "core")
    in_specs = (P(quad, ("y", "zh"), "x"), P(quad, None), P(quad), P(quad, None), P(None, ("y", "zh"), "x"), P(quad))
    out_specs = P(quad, ("y", "zh"), "x")
    return jax.shard_map(update, mesh=fine, in_specs=in_specs, out_specs=out_specs, check_vma=False)
```

```python
import itertools

import jax
import jax.numpy as jnp
from jax import lax
from jax.experimental import pallas as pl
from jax.experimental.pallas import tpu as pltpu
from jax.sharding import Mesh
from jax.sharding import PartitionSpec as P


STEP = 0.04
BF = jnp.bfloat16
F32 = jnp.float32
VM = pltpu.VMEM
OFFS = (0, -1, 1, 2)
ARRIVAL = tuple((o, i) for o, half in ((0, 0), (0, 2), (1, 0), (2, 0), (2, 2), (1, 2), (3, 0), (3, 2)) for i in (half, half + 1))
CHIPS = (0, 4, 2, 6, 1, 5, 3, 7)
ALL = ("zl", "core", "y", "zh", "x")
SPLIT = (8, 2, 4, 2, 4)


def shift(moves):
    every = list(itertools.product(*map(range, SPLIT)))
    number = {at: i for i, at in enumerate(every)}
    pairs = ((number[at], number.get(moves(*at))) for at in every)
    return [(i, j) for i, j in pairs if j is not None]


def plane_shift(phase, step):
    def moves(zl, core, y, zh, x):
        if (core + phase) % 2 == 0:
            return zl, core, y, zh, (x + step) % 4
        return zl, core, (y + step) % 4, zh, x

    return shift(moves)


def shape(dims, kind):
    return jax.ShapeDtypeStruct(dims, kind)


def halves(low, high):
    lane = lax.broadcasted_iota(jnp.int32, low.shape, 1)
    return jnp.where(lane < 64, low, high)


def swapped(x):
    return pltpu.roll(x, 64, 1)


def rows_kernel(modes_ref, logs_ref, out_ref, scr_ref, log_ref):
    scr_ref[...] = modes_ref[...].astype(F32)
    log_ref[...] = logs_ref[...]
    upper = jnp.zeros((1, 128), jnp.int32) + lax.axis_index("zh") == 0
    for k in range(2):
        logs = jnp.where(upper, log_ref[pl.ds(k, 8, stride=8), :], log_ref[pl.ds(6 + k, 8, stride=8), :])
        high = logs.astype(BF).astype(F32)
        block = jnp.where(upper, scr_ref[pl.ds(k, 64, stride=8), :], scr_ref[pl.ds(6 + k, 64, stride=8), :])
        out_ref[k * 80 : k * 80 + 80, :] = jnp.concatenate([block, high, logs - high], axis=0).astype(BF)


def channels_kernel(modes_ref, logs_ref, chan_ref, scr_ref, log_ref):
    scr_ref[...] = modes_ref[...].astype(F32)
    log_ref[...] = logs_ref[...]
    zeros = jnp.zeros((48, 128), F32)
    for y in range(8):
        block = scr_ref[pl.ds(y, 64, stride=8), :]
        logs = log_ref[pl.ds(y, 8, stride=8), :]
        high = logs.astype(BF).astype(F32)
        chan_ref[y] = jnp.concatenate([block, high, logs - high, zeros], axis=0).T


def edges_kernel(chan_ref, got_ref, full_ref, last_ref, lead_ref):
    lower = lax.axis_index("zh")
    zeros = jnp.zeros((48, 128), F32)
    got = got_ref[...].astype(F32)
    for k in range(2):
        full_ref[8 - 8 * lower + k, 8:136, :] = jnp.concatenate([got[k * 80 : k * 80 + 80], zeros], axis=0).T
    for r in range(8):
        full_ref[2 * lower + r, 8:136, :] = chan_ref[r]
    for r in range(10):
        last_ref[r * 8 : r * 8 + 8] = full_ref[r, 128:136, :].astype(BF)
        lead_ref[r * 8 : r * 8 + 8] = full_ref[r, 8:16, :].astype(BF)


def log_rows(cell_ref, rows):
    lane = lax.broadcasted_iota(jnp.int32, (rows, 128), 1)
    logs = jnp.zeros((rows, 128), F32)
    for g in range(8):
        piece = pltpu.roll(cell_ref[g * rows : (g + 1) * rows, :], (g * 16 - 64) % 128, 1)
        logs = jnp.where((lane >= g * 16) & (lane < g * 16 + 16), piece, logs)
    return logs


def patches_kernel(full_ref, left_ref, right_ref, pars_ref, send_ref, wide_ref, cell_ref, scr_ref):
    left, right = left_ref[...].astype(F32), right_ref[...].astype(F32)
    for r in range(10):
        wide_ref[r, 0:8, :] = left[r * 8 : r * 8 + 8]
        wide_ref[r, 8:136, :] = full_ref[r, 8:136, :]
        wide_ref[r, 136:144, :] = right[r * 8 : r * 8 + 8]
    zh = lax.axis_index("zh")
    scr_ref[...] = jnp.zeros_like(scr_ref)
    for d in range(8):
        for r in range(8):
            cell_ref[r * 20 : r * 20 + 20, :] = wide_ref[2 * zh + r, 16 * d + 6 : 16 * d + 26, :]
        scr_ref[0:80, :] = halves(cell_ref[0:80, :], swapped(cell_ref[80:160, :]))
        scr_ref[80:100, :] = log_rows(cell_ref, 20)
        send_ref[zh * 8 + d] = scr_ref[...].astype(BF)
    pars = pars_ref[...]
    high = pars.astype(BF).astype(F32)
    scr_ref[56:76, :] = high
    scr_ref[76:96, :] = pars - high
    for d in range(8):
        for r in range(4):
            cell_ref[r * 20 : r * 20 + 20, :] = wide_ref[6 - 6 * zh + r, 16 * d + 6 : 16 * d + 26, :]
        scr_ref[0:40, :] = halves(cell_ref[0:40, :], swapped(cell_ref[40:80, :]))
        scr_ref[40:50, :] = log_rows(cell_ref, 10)
        send_ref[8 - 8 * zh + d] = scr_ref[...].astype(BF)


def coef_kernel(mine_ref, coef_ref, wr_ref, scr_ref, par_ref, log_ref):
    core, y, zh, x = (lax.axis_index(axis) for axis in ("core", "y", "zh", "x"))
    zl = lax.axis_index("zl")
    for z in range(8):
        scr_ref[z * 40 : (z + 1) * 40, :] = mine_ref[8 - 8 * zh + (zl ^ CHIPS[z])].astype(F32)[56:96]
    sub = lax.broadcasted_iota(jnp.int32, (8, 128), 0)
    grp = lax.broadcasted_iota(jnp.int32, (8, 128), 1) // 16
    for v in range(10):
        for h in range(2):
            at = v * 2 + h
            got = scr_ref[pl.ds(at, 8, stride=40), :] + scr_ref[pl.ds(at + 20, 8, stride=40), :]
            for s in (1, 2, 4):
                up = pltpu.roll(pltpu.roll(got, 8 - s, 0), 16 * s, 1)
                down = pltpu.roll(pltpu.roll(got, s, 0), 128 - 16 * s, 1)
                mine, bit = (sub & s) > 0, (grp & s) > 0
                got = jnp.where(mine == bit, got, jnp.where(mine, down, up))
            par_ref[v, h * 8 : h * 8 + 8, :] = got
    same = mine_ref[zh * 8].astype(F32)
    same = same + pltpu.roll(same, 120, 1)
    other = mine_ref[8 - 8 * zh].astype(F32)
    other = other + pltpu.roll(other, 120, 1)
    for g in range(8):
        log_ref[40 + g * 20 : 60 + g * 20, :] = pltpu.roll(same, (128 - g * 16) % 128, 1)[80:100]
        at = g * 10 if g < 4 else 160 + g * 10
        log_ref[at : at + 10, :] = pltpu.roll(other, (128 - g * 16) % 128, 1)[40:50]
    cols = [log_ref[:, j : j + 1] for j in range(8)]
    for n, (o, i) in enumerate(ARRIVAL):
        dy, dx = jnp.where(core == 0, OFFS[o], OFFS[i]), jnp.where(core == 0, OFFS[i], OFFS[o])
        p = ((y + dy) & 3) * 4 + ((x + dx) & 3)
        for v in range(2):
            wr_ref[v, n : n + 1, :] = par_ref[v, pl.ds(p, 1), :]
        acc = cols[0] * par_ref[2, pl.ds(p, 1), :]
        for j in range(1, 8):
            acc = acc + cols[j] * par_ref[2 + j, pl.ds(p, 1), :]
        coef_ref[n] = jnp.exp(acc)


def state_kernel(mine_ref, theirs_ref, state_ref, scr_ref):
    first = jnp.zeros((1, 128), jnp.int32) + lax.axis_index("core") == 0
    zh = lax.axis_index("zh")
    for z in range(8):
        for at, rows, lo, hi in ((zh * 8 + z, 80, 40, 120), (8 - 8 * zh + z, 40, 0, 200)):
            mine, theirs = mine_ref[at].astype(F32)[0:rows], theirs_ref[at].astype(F32)[0:rows]
            zero, one = jnp.where(first, mine, theirs), jnp.where(first, theirs, mine)
            scr_ref[lo : lo + rows, :] = halves(zero, swapped(one))
            scr_ref[hi : hi + rows, :] = halves(swapped(zero), one)
        state_ref[:, z * 128 : (z + 1) * 128] = scr_ref[...].astype(BF)


def drive(f_ref, h, coef_ref, c, rows, skip, rate, weight):
    def f(d):
        return f_ref[h, 20 + d : 20 + d + rows, :]

    def k(d):
        return coef_ref[c, skip + 20 + d : skip + 20 + d + rows, :]

    mid, kmid = f(0), k(0)
    total = (kmid + k(-20)) * (f(-20) - mid)
    for d in (20, -1, 1):
        total = total + (kmid + k(d)) * (f(d) - mid)
    total = total + rate * (mid - mid * mid * mid)
    return (weight * total).astype(BF)


def sweep(state, basis_refs, coef_ref, wr_ref, f_ref, acc_ref, rows, skip, c=0):
    for ref in basis_refs:
        block = ref[...]
        field = lax.dot_general(state, block, (((1,), (1,)), ((), ())), preferred_element_type=F32)
        parts = []
        for h in range(2):
            f_ref[h, : field.shape[0], :] = field[:, h * 128 : (h + 1) * 128]
            weight, rate = wr_ref[0, c : c + 1, :], wr_ref[1, c : c + 1, :]
            parts.append(drive(f_ref, h, coef_ref, c, rows, skip, rate, weight))
            c += 1
        acc_ref[...] += jnp.dot(jnp.concatenate(parts, axis=1), block, preferred_element_type=F32)


def early_kernel(*refs):
    blocks, (state_ref, coef_ref, wr_ref, acc_ref, f_ref) = refs[:5], refs[5:]
    acc_ref[...] = jnp.zeros_like(acc_ref)
    sweep(state_ref[...], blocks, coef_ref, wr_ref, f_ref, acc_ref, 200, 0)


def late_kernel(*refs):
    blocks, (state_ref, coef_ref, wr_ref, sum_ref, out_ref, f_ref, acc_ref) = refs[:3], refs[3:]
    acc_ref[...] = sum_ref[...]
    sweep(state_ref[...], blocks, coef_ref, wr_ref, f_ref, acc_ref, 200, 0, 10)
    out_ref[...] = acc_ref[...].astype(BF)


def second_kernel(*refs):
    blocks, (state_ref, coef_ref, wr_ref, own_ref, other_ref, kept_ref, sent_ref, f_ref, acc_ref) = refs[:8], refs[8:]
    total = own_ref[...].astype(F32) + other_ref[...].astype(F32)
    now = state_ref[...].astype(F32)[20:220]
    cell = lax.broadcasted_iota(jnp.int32, (200, 128), 0).astype(F32)
    row = jnp.floor((cell + 0.5) * 0.05)
    col = cell - 20.0 * row
    zl, _, y, zh, x = (lax.axis_index(axis) for axis in ALL)
    low = jnp.where((y == 0) & (zh == 0), 1.0, 0.0)
    high = jnp.where((y == 3) & (zh == 1), 8.0, 9.0)
    left = jnp.where((x == 0) & (zl == 0), 2.0, 0.0)
    right = jnp.where((x == 3) & (zl == 7), 17.0, 19.0)
    inside = (row >= low) & (row <= high) & (col >= left) & (col <= right)
    keep = jnp.where(inside, 1.0, 0.0)[:, 0:1]
    state = ((now + STEP * total) * keep).astype(BF)
    acc_ref[...] = jnp.zeros_like(acc_ref)
    sweep(state, blocks, coef_ref, wr_ref, f_ref, acc_ref, 160, 20)
    first = jnp.zeros((1, 128), jnp.int32) + lax.axis_index("core") == 0
    for z in range(8):
        for y in range(4):
            low = acc_ref[y * 20 + 2 : y * 20 + 18, z * 128 : (z + 1) * 128]
            high = acc_ref[y * 20 + 82 : y * 20 + 98, z * 128 : (z + 1) * 128]
            zero, one = halves(low, swapped(high)), halves(swapped(low), high)
            kept_ref[z, y * 16 : y * 16 + 16, :] = jnp.where(first, zero, one)
            sent_ref[z, y * 16 : y * 16 + 16, :] = jnp.where(first, one, zero).astype(BF)


def add_kernel(kept_ref, got_ref, out_ref):
    out_ref[...] = (kept_ref[...] + got_ref[...].astype(F32)).astype(BF)


def finish_kernel(back_ref, modes_ref, out_ref, scr_ref):
    for y in range(4):
        parts = [
            back_ref[z, y * 16 : y * 16 + 16, :].astype(F32) for z in range(8)
        ]
        turned = jnp.concatenate(parts, axis=0).T
        scr_ref[pl.ds(y, 64, stride=8), :] = turned[0:64]
        scr_ref[pl.ds(y + 4, 64, stride=8), :] = turned[64:128]
    out_ref[...] = modes_ref[...].astype(F32) + STEP * scr_ref[...]


SMEM = pl.BlockSpec(memory_space=pltpu.SMEM)
WHOLE = pl.BlockSpec(memory_space=pltpu.VMEM)


def call(kernel, outs, scratch, scalars, *args):
    specs = [SMEM] * scalars + [WHOLE] * (len(args) - scalars)
    if kernel in (early_kernel, late_kernel, second_kernel):
        args = [pltpu.with_memory_space_constraint(a, pltpu.VMEM) if a.size >= 1 << 17 else a for a in args]
    single = not isinstance(outs, (list, tuple))
    return pl.pallas_call(
        kernel,
        out_shape=outs,
        in_specs=specs,
        out_specs=WHOLE if single else [WHOLE] * len(outs),
        scratch_shapes=scratch,
        compiler_params=pltpu.CompilerParams(vmem_limit_bytes=20 << 20),
    )(*args)


def update(modes_now, basis_rows, quad_weights, germ_nodes, log_fields, reaction_rates):
    y, x = lax.axis_index("y"), lax.axis_index("x")

    part = lax.dynamic_slice_in_dim(basis_rows, (y * 4 + x) * 16, 16, axis=0)
    shard = part
    for hop in (4, 2, 1):
        got = lax.ppermute(shard, "zl", [(i, i ^ hop) for i in range(8)])
        shard = jnp.concatenate([shard, got], axis=0)

    modes, logs = modes_now.reshape(512, 128), log_fields.reshape(64, 128)
    scratch = [VM((512, 128), F32), VM((64, 128), F32)]
    rows = call(rows_kernel, shape((160, 128), BF), scratch, 0, modes, logs)

    def toward(zl, core, y, zh, x):
        return zl, core, y + 2 * zh - 1, zh, x

    got = lax.ppermute(rows, ALL, shift(toward))
    chan = call(channels_kernel, shape((8, 128, 128), F32), scratch, 0, modes, logs)
    full, last, lead = call(
        edges_kernel,
        [shape((10, 144, 128), F32), shape((80, 128), BF), shape((80, 128), BF)],
        [],
        0,
        chan,
        got,
    )
    right = [(i, i + 1) for i in range(3)]
    from_left = lax.ppermute(last, "x", right)
    from_right = lax.ppermute(lead, "x", [(j, i) for i, j in right])
    pars = jnp.concatenate([quad_weights[None], reaction_rates[None], germ_nodes.T], axis=0).reshape(20, 128)
    patch = call(
        patches_kernel,
        shape((16, 104, 128), BF),
        [VM((10, 144, 128), F32), VM((160, 128), F32), VM((104, 128), F32)],
        0,
        full,
        from_left,
        from_right,
        pars,
    )
    mine = lax.all_to_all(patch, ("zh", "zl"), 0, 0, tiled=True)
    theirs = lax.ppermute(mine, "core", [(0, 1), (1, 0)])

    fwd, bwd = plane_shift(0, 1), plane_shift(0, -1)
    less = lax.ppermute(shard, ALL, fwd)
    more = lax.ppermute(shard, ALL, bwd)
    near = jnp.concatenate([shard, less], axis=0)
    far = lax.ppermute(shard, ALL, plane_shift(0, 2))
    fwd, bwd = plane_shift(1, 1), plane_shift(1, -1)
    near_less = lax.ppermute(near, ALL, fwd)
    near_more = lax.ppermute(near, ALL, bwd)
    away = jnp.concatenate([more, far], axis=0)
    away_more = lax.ppermute(away, ALL, bwd)
    away_less = lax.ppermute(away, ALL, fwd)
    near_far = lax.ppermute(near_less, ALL, fwd)
    away_far = lax.ppermute(away_more, ALL, bwd)
    blocks = (near, away, near_less, near_more, away_more, away_less, near_far, away_far)

    coef, wr = call(
        coef_kernel,
        [shape((16, 240, 128), F32), shape((2, 16, 128), F32)],
        [VM((320, 128), F32), VM((10, 16, 128), F32), VM((240, 128), F32)],
        0,
        mine,
    )
    state = call(state_kernel, shape((240, 1024), BF), [VM((240, 128), F32)], 0, mine, theirs)
    scratch = [VM((2, 240, 128), F32), VM((200, 1024), F32)]
    part = call(early_kernel, shape((200, 1024), F32), scratch[:1], 0, *blocks[:5], state, coef, wr)
    own = call(late_kernel, shape((200, 1024), BF), scratch, 0, *blocks[5:], state, coef, wr, part)
    other = lax.ppermute(own, "core", [(0, 1), (1, 0)])
    scratch = [VM((2, 200, 128), F32), VM((160, 1024), F32)]
    outs = [shape((8, 64, 128), F32), shape((8, 64, 128), BF)]
    kept, sent = call(second_kernel, outs, scratch, 0, *blocks, state, coef, wr, own, other)
    got = lax.ppermute(sent, "core", [(0, 1), (1, 0)])
    out = call(add_kernel, shape((8, 64, 128), BF), [], 0, kept, got)
    back = lax.all_to_all(out, "zl", 0, 0, tiled=True)
    result = call(finish_kernel, shape((512, 128), F32), [VM((512, 128), F32)], 0, back, modes)
    return result.reshape(64, 8, 128)


def solution(mesh):
    fine = Mesh(mesh.devices.reshape(SPLIT), ALL)
    quad = ("zl", "core")
    in_specs = (P(quad, ("y", "zh"), "x"), P(quad, None), P(quad), P(quad, None), P(None, ("y", "zh"), "x"), P(quad))
    out_specs = P(quad, ("y", "zh"), "x")
    return jax.shard_map(update, mesh=fine, in_specs=in_specs, out_specs=out_specs, check_vma=False)
```

```python
import itertools

import jax
import jax.numpy as jnp
from jax import lax
from jax.experimental import pallas as pl
from jax.experimental.pallas import tpu as pltpu
from jax.sharding import Mesh
from jax.sharding import PartitionSpec as P


STEP = 0.04
BF = jnp.bfloat16
F32 = jnp.float32
VM = pltpu.VMEM
OFFS = (0, -1, 1, 2)
ARRIVAL = tuple((o, i) for o, half in ((0, 0), (0, 2), (1, 0), (2, 0), (2, 2), (1, 2), (3, 0), (3, 2)) for i in (half, half + 1))
CHIPS = (0, 4, 2, 6, 1, 5, 3, 7)
ALL = ("zl", "core", "y", "zh", "x")
SPLIT = (8, 2, 4, 2, 4)


def shift(moves):
    every = list(itertools.product(*map(range, SPLIT)))
    number = {at: i for i, at in enumerate(every)}
    pairs = ((number[at], number.get(moves(*at))) for at in every)
    return [(i, j) for i, j in pairs if j is not None]


def plane_shift(phase, step):
    def moves(zl, core, y, zh, x):
        if (core + phase) % 2 == 0:
            return zl, core, y, zh, (x + step) % 4
        return zl, core, (y + step) % 4, zh, x

    return shift(moves)


def shape(dims, kind):
    return jax.ShapeDtypeStruct(dims, kind)


def halves(low, high):
    lane = lax.broadcasted_iota(jnp.int32, low.shape, 1)
    return jnp.where(lane < 64, low, high)


def swapped(x):
    return pltpu.roll(x, 64, 1)


def rows_kernel(modes_ref, logs_ref, out_ref, scr_ref, log_ref):
    scr_ref[...] = modes_ref[...].astype(F32)
    log_ref[...] = logs_ref[...]
    upper = jnp.zeros((1, 128), jnp.int32) + lax.axis_index("zh") == 0
    for k in range(2):
        logs = jnp.where(upper, log_ref[pl.ds(k, 8, stride=8), :], log_ref[pl.ds(6 + k, 8, stride=8), :])
        high = logs.astype(BF).astype(F32)
        block = jnp.where(upper, scr_ref[pl.ds(k, 64, stride=8), :], scr_ref[pl.ds(6 + k, 64, stride=8), :])
        out_ref[k * 80 : k * 80 + 80, :] = jnp.concatenate([block, high, logs - high], axis=0).astype(BF)


def channels_kernel(modes_ref, logs_ref, chan_ref, scr_ref, log_ref):
    scr_ref[...] = modes_ref[...].astype(F32)
    log_ref[...] = logs_ref[...]
    zeros = jnp.zeros((48, 128), F32)
    for y in range(8):
        block = scr_ref[pl.ds(y, 64, stride=8), :]
        logs = log_ref[pl.ds(y, 8, stride=8), :]
        high = logs.astype(BF).astype(F32)
        chan_ref[y] = jnp.concatenate([block, high, logs - high, zeros], axis=0).T


def edges_kernel(chan_ref, got_ref, full_ref, last_ref, lead_ref):
    lower = lax.axis_index("zh")
    zeros = jnp.zeros((48, 128), F32)
    got = got_ref[...].astype(F32)
    for k in range(2):
        full_ref[8 - 8 * lower + k, 8:136, :] = jnp.concatenate([got[k * 80 : k * 80 + 80], zeros], axis=0).T
    for r in range(8):
        full_ref[2 * lower + r, 8:136, :] = chan_ref[r]
    for r in range(10):
        last_ref[r * 8 : r * 8 + 8] = full_ref[r, 128:136, :].astype(BF)
        lead_ref[r * 8 : r * 8 + 8] = full_ref[r, 8:16, :].astype(BF)


def log_rows(cell_ref, rows):
    lane = lax.broadcasted_iota(jnp.int32, (rows, 128), 1)
    logs = jnp.zeros((rows, 128), F32)
    for g in range(8):
        piece = pltpu.roll(cell_ref[g * rows : (g + 1) * rows, :], (g * 16 - 64) % 128, 1)
        logs = jnp.where((lane >= g * 16) & (lane < g * 16 + 16), piece, logs)
    return logs


def patches_kernel(
    full_ref, left_ref, right_ref, weights_ref, rates_ref, nodes_ref, send_ref, wide_ref, cell_ref, scr_ref, pars_ref
):
    left, right = left_ref[...].astype(F32), right_ref[...].astype(F32)
    for r in range(10):
        wide_ref[r, 0:8, :] = left[r * 8 : r * 8 + 8]
        wide_ref[r, 8:136, :] = full_ref[r, 8:136, :]
        wide_ref[r, 136:144, :] = right[r * 8 : r * 8 + 8]
    zh = lax.axis_index("zh")
    scr_ref[...] = jnp.zeros_like(scr_ref)
    for d in range(8):
        for r in range(8):
            cell_ref[r * 20 : r * 20 + 20, :] = wide_ref[2 * zh + r, 16 * d + 6 : 16 * d + 26, :]
        scr_ref[0:80, :] = halves(cell_ref[0:80, :], swapped(cell_ref[80:160, :]))
        scr_ref[80:100, :] = log_rows(cell_ref, 20)
        send_ref[zh * 8 + d] = scr_ref[...].astype(BF)
    for h in range(2):
        half = slice(h * 128, h * 128 + 128)
        pars_ref[h : h + 1, :] = weights_ref[:, half]
        pars_ref[2 + h : 3 + h, :] = rates_ref[:, half]
        pars_ref[pl.ds(4 + h, 8, stride=2), :] = nodes_ref[:, half]
    pars = pars_ref[...]
    high = pars.astype(BF).astype(F32)
    scr_ref[56:76, :] = high
    scr_ref[76:96, :] = pars - high
    for d in range(8):
        for r in range(4):
            cell_ref[r * 20 : r * 20 + 20, :] = wide_ref[6 - 6 * zh + r, 16 * d + 6 : 16 * d + 26, :]
        scr_ref[0:40, :] = halves(cell_ref[0:40, :], swapped(cell_ref[40:80, :]))
        scr_ref[40:50, :] = log_rows(cell_ref, 10)
        send_ref[8 - 8 * zh + d] = scr_ref[...].astype(BF)


def coef_kernel(mine_ref, coef_ref, wr_ref, scr_ref, par_ref, log_ref):
    core, y, zh, x = (lax.axis_index(axis) for axis in ("core", "y", "zh", "x"))
    zl = lax.axis_index("zl")
    for z in range(8):
        scr_ref[z * 40 : (z + 1) * 40, :] = mine_ref[8 - 8 * zh + (zl ^ CHIPS[z])].astype(F32)[56:96]
    sub = lax.broadcasted_iota(jnp.int32, (8, 128), 0)
    grp = lax.broadcasted_iota(jnp.int32, (8, 128), 1) // 16
    for v in range(10):
        for h in range(2):
            at = v * 2 + h
            got = scr_ref[pl.ds(at, 8, stride=40), :] + scr_ref[pl.ds(at + 20, 8, stride=40), :]
            for s in (1, 2, 4):
                up = pltpu.roll(pltpu.roll(got, 8 - s, 0), 16 * s, 1)
                down = pltpu.roll(pltpu.roll(got, s, 0), 128 - 16 * s, 1)
                mine, bit = (sub & s) > 0, (grp & s) > 0
                got = jnp.where(mine == bit, got, jnp.where(mine, down, up))
            par_ref[v, h * 8 : h * 8 + 8, :] = got
    same = mine_ref[zh * 8].astype(F32)
    same = same + pltpu.roll(same, 120, 1)
    other = mine_ref[8 - 8 * zh].astype(F32)
    other = other + pltpu.roll(other, 120, 1)
    for g in range(8):
        log_ref[40 + g * 20 : 60 + g * 20, :] = pltpu.roll(same, (128 - g * 16) % 128, 1)[80:100]
        at = g * 10 if g < 4 else 160 + g * 10
        log_ref[at : at + 10, :] = pltpu.roll(other, (128 - g * 16) % 128, 1)[40:50]
    cols = [log_ref[:, j : j + 1] for j in range(8)]
    for n, (o, i) in enumerate(ARRIVAL):
        dy, dx = jnp.where(core == 0, OFFS[o], OFFS[i]), jnp.where(core == 0, OFFS[i], OFFS[o])
        p = ((y + dy) & 3) * 4 + ((x + dx) & 3)
        for v in range(2):
            wr_ref[v, n : n + 1, :] = par_ref[v, pl.ds(p, 1), :]
        acc = cols[0] * par_ref[2, pl.ds(p, 1), :]
        for j in range(1, 8):
            acc = acc + cols[j] * par_ref[2 + j, pl.ds(p, 1), :]
        coef_ref[n] = jnp.exp(acc)


def state_kernel(mine_ref, theirs_ref, state_ref, scr_ref):
    first = jnp.zeros((1, 128), jnp.int32) + lax.axis_index("core") == 0
    zh = lax.axis_index("zh")
    for z in range(8):
        for at, rows, lo, hi in ((zh * 8 + z, 80, 40, 120), (8 - 8 * zh + z, 40, 0, 200)):
            mine, theirs = mine_ref[at].astype(F32)[0:rows], theirs_ref[at].astype(F32)[0:rows]
            zero, one = jnp.where(first, mine, theirs), jnp.where(first, theirs, mine)
            scr_ref[lo : lo + rows, :] = halves(zero, swapped(one))
            scr_ref[hi : hi + rows, :] = halves(swapped(zero), one)
        state_ref[:, z * 128 : (z + 1) * 128] = scr_ref[...].astype(BF)


def drive(f_ref, h, coef_ref, c, rows, skip, rate, weight):
    def f(d):
        return f_ref[h, 20 + d : 20 + d + rows, :]

    def k(d):
        return coef_ref[c, skip + 20 + d : skip + 20 + d + rows, :]

    mid, kmid = f(0), k(0)
    total = (kmid + k(-20)) * (f(-20) - mid)
    for d in (20, -1, 1):
        total = total + (kmid + k(d)) * (f(d) - mid)
    total = total + rate * (mid - mid * mid * mid)
    return (weight * total).astype(BF)


def sweep(state, basis_refs, coef_ref, wr_ref, f_ref, acc_ref, rows, skip, c=0):
    for ref in basis_refs:
        block = ref[...]
        field = lax.dot_general(state, block, (((1,), (1,)), ((), ())), preferred_element_type=F32)
        parts = []
        for h in range(2):
            f_ref[h, : field.shape[0], :] = field[:, h * 128 : (h + 1) * 128]
            weight, rate = wr_ref[0, c : c + 1, :], wr_ref[1, c : c + 1, :]
            parts.append(drive(f_ref, h, coef_ref, c, rows, skip, rate, weight))
            c += 1
        acc_ref[...] += jnp.dot(jnp.concatenate(parts, axis=1), block, preferred_element_type=F32)


def early_kernel(*refs):
    blocks, (state_ref, coef_ref, wr_ref, acc_ref, f_ref) = refs[:5], refs[5:]
    acc_ref[...] = jnp.zeros_like(acc_ref)
    sweep(state_ref[...], blocks, coef_ref, wr_ref, f_ref, acc_ref, 200, 0)


def late_kernel(*refs):
    blocks, (state_ref, coef_ref, wr_ref, sum_ref, out_ref, f_ref, acc_ref) = refs[:3], refs[3:]
    acc_ref[...] = sum_ref[...]
    sweep(state_ref[...], blocks, coef_ref, wr_ref, f_ref, acc_ref, 200, 0, 10)
    out_ref[...] = acc_ref[...].astype(BF)


def second_kernel(*refs):
    blocks, (state_ref, coef_ref, wr_ref, own_ref, other_ref, kept_ref, sent_ref, f_ref, acc_ref) = refs[:8], refs[8:]
    total = own_ref[...].astype(F32) + other_ref[...].astype(F32)
    now = state_ref[...].astype(F32)[20:220]
    cell = lax.broadcasted_iota(jnp.int32, (200, 128), 0).astype(F32)
    row = jnp.floor((cell + 0.5) * 0.05)
    col = cell - 20.0 * row
    zl, _, y, zh, x = (lax.axis_index(axis) for axis in ALL)
    low = jnp.where((y == 0) & (zh == 0), 1.0, 0.0)
    high = jnp.where((y == 3) & (zh == 1), 8.0, 9.0)
    left = jnp.where((x == 0) & (zl == 0), 2.0, 0.0)
    right = jnp.where((x == 3) & (zl == 7), 17.0, 19.0)
    inside = (row >= low) & (row <= high) & (col >= left) & (col <= right)
    keep = jnp.where(inside, 1.0, 0.0)[:, 0:1]
    state = ((now + STEP * total) * keep).astype(BF)
    acc_ref[...] = jnp.zeros_like(acc_ref)
    sweep(state, blocks, coef_ref, wr_ref, f_ref, acc_ref, 160, 20)
    first = jnp.zeros((1, 128), jnp.int32) + lax.axis_index("core") == 0
    for z in range(8):
        for y in range(4):
            low = acc_ref[y * 20 + 2 : y * 20 + 18, z * 128 : (z + 1) * 128]
            high = acc_ref[y * 20 + 82 : y * 20 + 98, z * 128 : (z + 1) * 128]
            zero, one = halves(low, swapped(high)), halves(swapped(low), high)
            kept_ref[z, y * 16 : y * 16 + 16, :] = jnp.where(first, zero, one)
            sent_ref[z, y * 16 : y * 16 + 16, :] = jnp.where(first, one, zero).astype(BF)


def add_kernel(kept_ref, got_ref, out_ref):
    out_ref[...] = (kept_ref[...] + got_ref[...].astype(F32)).astype(BF)


def finish_kernel(back_ref, modes_ref, out_ref, scr_ref):
    for y in range(4):
        parts = [
            back_ref[z, y * 16 : y * 16 + 16, :].astype(F32) for z in range(8)
        ]
        turned = jnp.concatenate(parts, axis=0).T
        scr_ref[pl.ds(y, 64, stride=8), :] = turned[0:64]
        scr_ref[pl.ds(y + 4, 64, stride=8), :] = turned[64:128]
    out_ref[...] = modes_ref[...].astype(F32) + STEP * scr_ref[...]


SMEM = pl.BlockSpec(memory_space=pltpu.SMEM)
WHOLE = pl.BlockSpec(memory_space=pltpu.VMEM)


def call(kernel, outs, scratch, scalars, *args):
    specs = [SMEM] * scalars + [WHOLE] * (len(args) - scalars)
    if kernel in (early_kernel, late_kernel, second_kernel):
        args = [pltpu.with_memory_space_constraint(a, pltpu.VMEM) if a.size >= 1 << 17 else a for a in args]
    single = not isinstance(outs, (list, tuple))
    return pl.pallas_call(
        kernel,
        out_shape=outs,
        in_specs=specs,
        out_specs=WHOLE if single else [WHOLE] * len(outs),
        scratch_shapes=scratch,
        compiler_params=pltpu.CompilerParams(vmem_limit_bytes=20 << 20),
    )(*args)


def update(modes_now, basis_rows, quad_weights, germ_nodes, log_fields, reaction_rates):
    y, x = lax.axis_index("y"), lax.axis_index("x")

    part = lax.dynamic_slice_in_dim(basis_rows, (y * 4 + x) * 16, 16, axis=0)
    shard = part
    for hop in (4, 2, 1):
        got = lax.ppermute(shard, "zl", [(i, i ^ hop) for i in range(8)])
        shard = jnp.concatenate([shard, got], axis=0)

    modes, logs = modes_now.reshape(512, 128), log_fields.reshape(64, 128)
    scratch = [VM((512, 128), F32), VM((64, 128), F32)]
    rows = call(rows_kernel, shape((160, 128), BF), scratch, 0, modes, logs)

    def toward(zl, core, y, zh, x):
        return zl, core, y + 2 * zh - 1, zh, x

    got = lax.ppermute(rows, ALL, shift(toward))
    chan = call(channels_kernel, shape((8, 128, 128), F32), scratch, 0, modes, logs)
    full, last, lead = call(
        edges_kernel,
        [shape((10, 144, 128), F32), shape((80, 128), BF), shape((80, 128), BF)],
        [],
        0,
        chan,
        got,
    )
    right = [(i, i + 1) for i in range(3)]
    from_left = lax.ppermute(last, "x", right)
    from_right = lax.ppermute(lead, "x", [(j, i) for i, j in right])
    patch = call(
        patches_kernel,
        shape((16, 104, 128), BF),
        [VM((10, 144, 128), F32), VM((160, 128), F32), VM((104, 128), F32), VM((20, 128), F32)],
        0,
        full,
        from_left,
        from_right,
        quad_weights[None],
        reaction_rates[None],
        germ_nodes.T,
    )
    mine = lax.all_to_all(patch, ("zh", "zl"), 0, 0, tiled=True)
    theirs = lax.ppermute(mine, "core", [(0, 1), (1, 0)])

    fwd, bwd = plane_shift(0, 1), plane_shift(0, -1)
    less = lax.ppermute(shard, ALL, fwd)
    more = lax.ppermute(shard, ALL, bwd)
    near = jnp.concatenate([shard, less], axis=0)
    far = lax.ppermute(less, ALL, fwd)
    fwd, bwd = plane_shift(1, 1), plane_shift(1, -1)
    near_less = lax.ppermute(near, ALL, fwd)
    near_more = lax.ppermute(near, ALL, bwd)
    away = jnp.concatenate([more, far], axis=0)
    away_more = lax.ppermute(away, ALL, bwd)
    away_less = lax.ppermute(away, ALL, fwd)
    near_far = lax.ppermute(near_less, ALL, fwd)
    away_far = lax.ppermute(away_more, ALL, bwd)
    blocks = (near, away, near_less, near_more, away_more, away_less, near_far, away_far)

    coef, wr = call(
        coef_kernel,
        [shape((16, 240, 128), F32), shape((2, 16, 128), F32)],
        [VM((320, 128), F32), VM((10, 16, 128), F32), VM((240, 128), F32)],
        0,
        mine,
    )
    state = call(state_kernel, shape((240, 1024), BF), [VM((240, 128), F32)], 0, mine, theirs)
    scratch = [VM((2, 240, 128), F32), VM((200, 1024), F32)]
    part = call(early_kernel, shape((200, 1024), F32), scratch[:1], 0, *blocks[:5], state, coef, wr)
    own = call(late_kernel, shape((200, 1024), BF), scratch, 0, *blocks[5:], state, coef, wr, part)
    other = lax.ppermute(own, "core", [(0, 1), (1, 0)])
    scratch = [VM((2, 200, 128), F32), VM((160, 1024), F32)]
    outs = [shape((8, 64, 128), F32), shape((8, 64, 128), BF)]
    kept, sent = call(second_kernel, outs, scratch, 0, *blocks, state, coef, wr, own, other)
    got = lax.ppermute(sent, "core", [(0, 1), (1, 0)])
    out = call(add_kernel, shape((8, 64, 128), BF), [], 0, kept, got)
    back = lax.all_to_all(out, "zl", 0, 0, tiled=True)
    result = call(finish_kernel, shape((512, 128), F32), [VM((512, 128), F32)], 0, back, modes)
    return result.reshape(64, 8, 128)


def solution(mesh):
    fine = Mesh(mesh.devices.reshape(SPLIT), ALL)
    quad = ("zl", "core")
    in_specs = (P(quad, ("y", "zh"), "x"), P(quad, None), P(quad), P(quad, None), P(None, ("y", "zh"), "x"), P(quad))
    out_specs = P(quad, ("y", "zh"), "x")
    return jax.shard_map(update, mesh=fine, in_specs=in_specs, out_specs=out_specs, check_vma=False)
```
